128 devices in a mesh: dom: 16 (over y, z), grp: 8 (over x, core).
Axes of the slice: x: 4, y: 4, z: 4, core: 2. Of those that a mesh axis runs over, the one named last changes fastest.
Arguments:
- a_strips: bfloat16 [4096, 64, 448], P(('dom', 'grp')), may hold values from -0.25 to 0.25
- p_strips: bfloat16 [4096, 64, 256], P(('dom', 'grp')), may hold values from -1.1953125 to 1.1953125
- nbr_local: int32 [4096, 7], P(('dom', 'grp')), may hold values from 0 to 79, as said below
- ap_slot: int32 [4096, 7, 4], P(('dom', 'grp')), may hold values from 0 to 7, as said below
- tile_slot: int32 [4096, 4, 8], P(('dom', 'grp')), may hold values from 0 to 71, as said below
- send_rows: int32 [128, 8, 6], P(('dom', 'grp')), may hold values from 0 to 31
- owner_map: int32 [128, 72], P(('dom', 'grp')), may hold values from 0 to 127
Outputs:
- coarse_tiles: float32 [64, 1048576], P(None, ('dom', 'grp'))
The draws below stay inside these ranges and needn't reach their ends.
Inputs may be any that keep to these rules, and one draw needn't show every extreme that they name: `nbr_local`: column 0 is the element itself. A value below 32 is an element of the same device; the value 32 + p * 6 + g stands for the row that neighbour p sends to this device in slot g, and every such ghost value appears on every device. `ap_slot`: each row's 7 * 4 entries name every value from 0 to 7. `tile_slot`: on every device each of the 72 partial tiles is named by some entry.
All inputs are finite; a program needn't handle non-finite values.
Results may differ from the reference program's by a relative error of at most 0.0029.
Values may be sent and summed in bfloat16 or wider, within the bound.
A program may use at most 192 MiB of HBM per device.

```python
import math
import jax
import jax.numpy as jnp
from jax import lax

KB = 64
KC = 64
NB = 7
PN = 4
QN = 8
E_DEV = 32
GCAP = 6
SCAP = 8
OWN = 128
NE = 4096
NGHOST = 48
LT = 72
N_DOM = 16
N_GRP = 8


def draw_nbr_local(key, part):
    devices = NE // E_DEV
    positions = E_DEV * (NB - 1)
    row_keys = jax.random.split(jax.random.fold_in(key, 11), devices)

    def per_device(device_key):
        first_key, second_key = jax.random.split(device_key)
        shuffled = jax.random.permutation(first_key, positions)
        local_rows = jax.random.randint(second_key, (positions,), 0, E_DEV)
        picked = jnp.where(shuffled < NGHOST, E_DEV + shuffled, local_rows)
        return picked.reshape(E_DEV, NB - 1)
    others = jax.vmap(per_device)(row_keys).reshape(NE, NB - 1)
    self_col = (jnp.arange(NE) % E_DEV)[:, None]
    return jnp.concatenate([self_col, others], 1).astype(jnp.int32)


def draw_ap_slot(key, part):
    row_keys = jax.random.split(jax.random.fold_in(key, 23), NE)

    def per_row(row_key):
        return (jax.random.permutation(row_key, NB * PN) % QN).reshape(NB, PN)
    return jax.vmap(per_row)(row_keys).astype(jnp.int32)


def draw_tile_slot(key, part):
    devices = NE // E_DEV
    positions = E_DEV * PN * QN
    row_keys = jax.random.split(jax.random.fold_in(key, 37), devices)

    def per_device(device_key):
        first_key, second_key = jax.random.split(device_key)
        shuffled = jax.random.permutation(first_key, positions)
        spread = jax.random.randint(second_key, (positions,), 0, LT)
        picked = jnp.where(shuffled < LT, shuffled, spread)
        return picked.reshape(E_DEV, PN, QN)
    return jax.vmap(per_device)(row_keys).reshape(NE, PN, QN).astype(jnp.int32)


def draw_send_rows(key, part):
    devices = NE // E_DEV
    picked = jax.random.randint(jax.random.fold_in(key, 41), (devices, 8, GCAP), 0, E_DEV)
    picked = picked.at[:, 0, 0].set(E_DEV - 1).at[:, 1, 0].set(0)
    return picked.astype(jnp.int32)


def draw_owner_map(key, part):
    devices = NE // E_DEV
    picked = jax.random.randint(jax.random.fold_in(key, 53), (devices, LT), 0, OWN)
    picked = picked.at[:, 0].set(OWN - 1).at[:, 1].set(0)
    return picked.astype(jnp.int32)


def level_of(rng, shape, pieces, smallest, largest):
    def one(axis_at, parts):
        steps = jax.random.uniform(jax.random.fold_in(jax.random.fold_in(rng, 6), axis_at), (parts,), jnp.float32, smallest / len(pieces), largest / len(pieces))
        return jnp.repeat(jnp.exp(steps), shape[axis_at] // parts).reshape((-1,) + (1,) * (len(shape) - axis_at - 1))

    factor_of = one(*pieces[0])
    for cut in pieces[1:]:
        factor_of = factor_of * one(*cut)
    return factor_of


def scatter_about(stream_key, dims, width, most, cuts=(), kind=jnp.bfloat16):
    values = width * jax.random.normal(stream_key, dims, jnp.float32)
    if cuts:
        values = values * level_of(stream_key, dims, cuts, -0.22, 0.18)
    return jnp.clip(values, -most, most).astype(kind)


def setup_inputs(seed: int = 0) -> dict:
    key_of = jax.random.split(jax.random.key(seed), 8)
    return {
        "a_strips": scatter_about(key_of[0], (NE, KB, NB * KB), (NB * KB) ** -0.5, 0.25, ((0, 128),)),
        "p_strips": scatter_about(key_of[1], (NE, KB, PN * KC), 0.2, 1.1953125, ((0, 128),)),
        "nbr_local": draw_nbr_local(jax.random.fold_in(key_of[7], 71), 0),
        "ap_slot": draw_ap_slot(jax.random.fold_in(key_of[7], 71), 0),
        "tile_slot": draw_tile_slot(jax.random.fold_in(key_of[7], 71), 0),
        "send_rows": draw_send_rows(jax.random.fold_in(key_of[7], 71), 0),
        "owner_map": draw_owner_map(jax.random.fold_in(key_of[7], 71), 0),
    }


def element_terms(a_block, p_block, nbr_block, slot_block, extended):
    block_len = a_block.shape[0]
    a_tiles = a_block.reshape(block_len, KB, NB, KB).astype(jnp.float32)
    gathered = extended[nbr_block].astype(jnp.float32)
    product = jnp.einsum("eijm,ejmn->ejin", a_tiles, gathered, precision=lax.Precision.HIGHEST)
    product = product.reshape(block_len, NB, KB, PN, KC)
    selector = (slot_block[..., None] == jnp.arange(QN, dtype=jnp.int32)).astype(jnp.float32)
    applied = jnp.einsum("ejikc,ejkq->eiqc", product, selector, precision=lax.Precision.HIGHEST)
    applied = lax.optimization_barrier(applied.astype(jnp.bfloat16)).astype(jnp.float32)
    own_tiles = p_block.reshape(block_len, KB, PN, KC).astype(jnp.float32)
    return jnp.einsum("emkc,emqd->ekqcd", own_tiles, applied, precision=lax.Precision.HIGHEST)


def reference(a_strips, p_strips, nbr_local, ap_slot, tile_slot, send_rows, owner_map):
    devices = N_DOM * N_GRP
    tiles_total = 9 * SCAP
    block_len = math.gcd(E_DEV, 32)
    blocks = E_DEV // block_len
    off_rows = jnp.array([-1, -1, -1, 0, 0, 1, 1, 1], dtype=jnp.int32)
    off_cols = jnp.array([-1, 0, 1, -1, 1, -1, 0, 1], dtype=jnp.int32)
    cell_rows = jnp.arange(9, dtype=jnp.int32) // 3 - 1
    cell_cols = jnp.arange(9, dtype=jnp.int32) % 3 - 1

    def per_device(coarse, device):
        dom_at = device // N_GRP
        grp_at = device % N_GRP
        first_row = device * E_DEV
        a_dev = lax.dynamic_slice_in_dim(a_strips, first_row, E_DEV, 0)
        p_dev = lax.dynamic_slice_in_dim(p_strips, first_row, E_DEV, 0)
        nbr_dev = lax.dynamic_slice_in_dim(nbr_local, first_row, E_DEV, 0)
        slot_dev = lax.dynamic_slice_in_dim(ap_slot, first_row, E_DEV, 0)
        tile_dev = lax.dynamic_slice_in_dim(tile_slot, first_row, E_DEV, 0)
        peers = ((dom_at + off_rows) % N_DOM) * N_GRP + (grp_at + off_cols) % N_GRP
        peer_rows = send_rows[peers, 7 - jnp.arange(8, dtype=jnp.int32)]
        sources = (peers[:, None] * E_DEV + peer_rows).reshape(-1)
        extended = jnp.concatenate([p_dev, p_strips[sources]], 0)

        def regroup(source_array):
            return source_array.reshape((blocks, block_len) + source_array.shape[1:])

        def accumulate(partial_value, inputs):
            a_block, p_block, nbr_block, slot_block, tile_block = inputs
            terms = element_terms(a_block, p_block, nbr_block, slot_block, extended)
            partial_value = partial_value.at[tile_block.reshape(-1)].add(terms.reshape(-1, KC, KC))
            return partial_value, None

        initial = jnp.zeros((tiles_total, KC, KC), jnp.float32)
        partial_value = lax.scan(accumulate, initial, (regroup(a_dev), regroup(p_dev), regroup(nbr_dev), regroup(slot_dev), regroup(tile_dev)))[0]
        parcels = partial_value.reshape(9, SCAP, KC, KC)
        owners = ((dom_at + cell_rows) % N_DOM) * N_GRP + (grp_at + cell_cols) % N_GRP
        maps = owner_map[owners].reshape(9, 9, SCAP)
        cells = jnp.arange(9, dtype=jnp.int32)
        targets = maps[cells, 8 - cells]
        coarse = coarse.at[owners[:, None], targets].add(parcels)
        return coarse, None

    coarse = jnp.zeros((devices, OWN, KC, KC), jnp.float32)
    coarse = lax.scan(per_device, coarse, jnp.arange(devices, dtype=jnp.int32))[0]
    return coarse.transpose(2, 0, 1, 3).reshape(KC, devices * OWN * KC)
```

```python
import jax
import jax.numpy as jnp
from jax import lax
from jax.experimental import pallas as pl
from jax.experimental.pallas import tpu as pltpu
from jax.sharding import PartitionSpec as P

KB = 64
KC = 64
NB = 7
PN = 4
QN = 8
OWN = 128
MESH = pl.DeviceIdType.MESH
CELLS = [(a, b) for a in (-1, 0, 1) for b in (-1, 0, 1)]
AROUND = [cell for cell in CELLS if cell != (0, 0)]
ORDER = sorted(range(8), key=lambda p: -(abs(AROUND[p][0]) * 2 + abs(AROUND[p][1])))


def device_at(offset):
    rows, cols = lax.axis_size("dom"), lax.axis_size("grp")
    i = lax.rem(lax.axis_index("dom") + offset[0] + rows, rows)
    j = lax.rem(lax.axis_index("grp") + offset[1] + cols, cols)
    return (i, j)


def greet():
    barrier = pltpu.get_barrier_semaphore()
    for offset in AROUND:
        pl.semaphore_signal(barrier, inc=1, device_id=device_at(offset), device_id_type=MESH)
    return barrier


def ghost_kernel(send_rows, p_ref, ghost_ref, outbox, send_sem, recv_sem):
    slots = send_rows.shape[0]
    barrier = greet()
    for p in ORDER:
        for g in range(slots):
            outbox[p * slots + g] = p_ref[send_rows[g, 0, p]]
    pl.semaphore_wait(barrier, 8)
    copies = []
    for p in ORDER:
        copies.append(
            pltpu.make_async_remote_copy(
                src_ref=outbox.at[pl.ds(p * slots, slots)],
                dst_ref=ghost_ref.at[pl.ds((7 - p) * slots, slots)],
                send_sem=send_sem.at[p],
                recv_sem=recv_sem.at[7 - p],
                device_id=device_at(AROUND[p]),
                device_id_type=MESH,
            )
        )
        copies[-1].start()
    for copy in copies:
        copy.wait()


def local_kernel(
    nbr, ap, ts, a_ref, p_hbm, g_hbm, out_ref, ext, acc_a, acc_b, part_a, part_b, part_c, part_d, sem
):
    n = a_ref.shape[0]
    own = pltpu.make_async_copy(p_hbm, ext.at[pl.ds(0, n)], sem.at[0])
    ghosts = pltpu.make_async_copy(g_hbm, ext.at[pl.ds(n, g_hbm.shape[0])], sem.at[1])
    own.start()
    ghosts.start()
    parts = (part_a, part_b, part_c, part_d)
    for part in parts:
        part[...] = jnp.zeros_like(part)
    own.wait()
    ghosts.wait()
    low = lax.broadcasted_iota(jnp.int32, (KB, 128), 1) < KC

    def element(e, carry):
        acc_a[...] = jnp.zeros_like(acc_a)
        acc_b[...] = jnp.zeros_like(acc_b)
        for j in range(NB):
            x = ext[nbr[j, e]]
            prod = jnp.dot(a_ref[e, :, j * KB : (j + 1) * KB], x, preferred_element_type=jnp.float32)
            for half in range(2):
                chunk = prod[:, half * 128 : (half + 1) * 128]
                acc_a[ap[j, 2 * half, e]] += chunk
                acc_b[ap[j, 2 * half + 1, e]] += chunk
        columns = []
        for u in range(QN // 2):
            even = jnp.where(low, acc_a[2 * u], acc_b[2 * u])
            odd = jnp.where(low, acc_a[2 * u + 1], acc_b[2 * u + 1])
            even = even + pltpu.roll(even, KC, 1)
            odd = odd + pltpu.roll(odd, KC, 1)
            columns.append(jnp.where(low, even, odd).astype(jnp.bfloat16))
        applied = jnp.concatenate(columns, axis=1)
        contrib = lax.dot_general(
            ext[e], applied, (((0,), (0,)), ((), ())), preferred_element_type=jnp.float32
        )
        for k in range(PN):
            first, second = parts[:2] if k % 2 == 0 else parts[2:]
            for u in range(QN // 2):
                chunk = contrib[k * KC : (k + 1) * KC, u * 128 : (u + 1) * 128]
                first[ts[k, 2 * u, e]] += chunk
                second[ts[k, 2 * u + 1, e]] += chunk
        return carry

    lax.fori_loop(0, n, element, 0)

    def tile(t):
        total = jnp.where(low, part_a[t] + part_c[t], part_b[t] + part_d[t])
        return total + pltpu.roll(total, KC, 1)

    def pack(i, carry):
        out_ref[i] = jnp.where(low, tile(2 * i), tile(2 * i + 1)).astype(jnp.bfloat16)
        return carry

    lax.fori_loop(0, out_ref.shape[0], pack, 0)


def parcel_kernel(tiles_ref, returned_ref, send_sem, recv_sem, own_sem):
    pairs = tiles_ref.shape[0] // 9
    barrier = greet()
    own = pltpu.make_async_copy(
        tiles_ref.at[pl.ds(4 * pairs, pairs)], returned_ref.at[pl.ds(4 * pairs, pairs)], own_sem
    )
    own.start()
    pl.semaphore_wait(barrier, 8)
    copies = []
    for p in ORDER:
        cell = CELLS.index(AROUND[p])
        copies.append(
            pltpu.make_async_remote_copy(
                src_ref=tiles_ref.at[pl.ds(cell * pairs, pairs)],
                dst_ref=returned_ref.at[pl.ds((8 - cell) * pairs, pairs)],
                send_sem=send_sem.at[p],
                recv_sem=recv_sem.at[7 - p],
                device_id=device_at(AROUND[p]),
                device_id_type=MESH,
            )
        )
        copies[-1].start()
    own.wait()
    for copy in copies:
        copy.wait()


def owner_kernel(owner_map, returned_ref, out_ref):
    out_ref[...] = jnp.zeros_like(out_ref)
    low = lax.broadcasted_iota(jnp.int32, (KC, 128), 1) < KC

    def add(i, carry):
        pair = returned_ref[i].astype(jnp.float32)
        turned = pltpu.roll(pair, KC, 1)
        for side, same, other in ((0, pair, turned), (1, turned, pair)):
            m = owner_map[0, 2 * i + side]
            at = pl.ds(pl.multiple_of((m // 2) * 128, 128), 128)
            even = lax.rem(m, 2) == 0
            keep = jnp.logical_xor(low, jnp.logical_not(even))
            value = jnp.where(low, same, other)
            out_ref[:, at] += jnp.where(keep, value, 0.0)
        return carry

    lax.fori_loop(0, returned_ref.shape[0], add, 0)


def body(a_strips, p_strips, nbr_local, ap_slot, tile_slot, send_rows, owner_map):
    width = p_strips.shape[2]
    slots = send_rows.shape[2]
    smem = pl.BlockSpec(memory_space=pltpu.SMEM)
    vmem = pl.BlockSpec(memory_space=pltpu.VMEM)
    anywhere = pl.BlockSpec(memory_space=pl.ANY)
    tiles_total = owner_map.shape[1]
    n = a_strips.shape[0]
    ghosts = pl.pallas_call(
        ghost_kernel,
        out_shape=jax.ShapeDtypeStruct((8 * slots, KB, width), jnp.bfloat16),
        in_specs=[smem, vmem],
        out_specs=anywhere,
        scratch_shapes=[
            pltpu.VMEM((8 * slots, KB, width), jnp.bfloat16),
            pltpu.SemaphoreType.DMA((8,)),
            pltpu.SemaphoreType.DMA((8,)),
        ],
        compiler_params=pltpu.CompilerParams(collective_id=0, has_side_effects=True),
    )(send_rows.transpose(2, 0, 1), p_strips)
    tiles = pl.pallas_call(
        local_kernel,
        out_shape=jax.ShapeDtypeStruct((tiles_total // 2, KC, 2 * KC), jnp.bfloat16),
        in_specs=[smem, smem, smem, vmem, anywhere, anywhere],
        out_specs=vmem,
        scratch_shapes=[
            pltpu.VMEM((n + 8 * slots, KB, width), jnp.bfloat16),
            pltpu.VMEM((QN, KB, 2 * KC), jnp.float32),
            pltpu.VMEM((QN, KB, 2 * KC), jnp.float32),
        ]
        + [pltpu.VMEM((tiles_total, KC, 2 * KC), jnp.float32)] * 4
        + [pltpu.SemaphoreType.DMA((2,))],
    )(
        nbr_local.transpose(1, 0),
        ap_slot.transpose(1, 2, 0),
        tile_slot.transpose(1, 2, 0),
        a_strips,
        p_strips,
        ghosts,
    )
    returned = pl.pallas_call(
        parcel_kernel,
        out_shape=jax.ShapeDtypeStruct(tiles.shape, tiles.dtype),
        in_specs=[vmem],
        out_specs=vmem,
        scratch_shapes=[
            pltpu.SemaphoreType.DMA((8,)),
            pltpu.SemaphoreType.DMA((8,)),
            pltpu.SemaphoreType.DMA,
        ],
        compiler_params=pltpu.CompilerParams(collective_id=1, has_side_effects=True),
    )(tiles)
    return pl.pallas_call(
        owner_kernel,
        out_shape=jax.ShapeDtypeStruct((KC, OWN * KC), jnp.float32),
        in_specs=[smem, vmem],
        out_specs=vmem,
    )(owner_map, returned)


def solution(mesh):
    placed = (
        P(("dom", "grp"), None, None),
        P(("dom", "grp"), None, None),
        P(("dom", "grp"), None),
        P(("dom", "grp"), None, None),
        P(("dom", "grp"), None, None),
        P(("dom", "grp"), None, None),
        P(("dom", "grp"), None),
    )
    return jax.shard_map(
        body, mesh=mesh, in_specs=placed, out_specs=P(None, ("dom", "grp")), check_vma=False
    )
```

```python
import jax
import jax.numpy as jnp
from jax import lax
from jax.experimental import pallas as pl
from jax.experimental.pallas import tpu as pltpu
from jax.sharding import PartitionSpec as P

KB = 64
KC = 64
NB = 7
PN = 4
QN = 8
OWN = 128
GROUP = 4
MESH = pl.DeviceIdType.MESH
CELLS = [(a, b) for a in (-1, 0, 1) for b in (-1, 0, 1)]
AROUND = [cell for cell in CELLS if cell != (0, 0)]
ORDER = sorted(range(8), key=lambda p: -(abs(AROUND[p][0]) * 2 + abs(AROUND[p][1])))


def device_at(offset):
    rows, cols = lax.axis_size("dom"), lax.axis_size("grp")
    i = lax.rem(lax.axis_index("dom") + offset[0] + rows, rows)
    j = lax.rem(lax.axis_index("grp") + offset[1] + cols, cols)
    return (i, j)


def greet():
    barrier = pltpu.get_barrier_semaphore()
    for offset in AROUND:
        pl.semaphore_signal(barrier, inc=1, device_id=device_at(offset), device_id_type=MESH)
    return barrier


def folded(x):
    turned = x.T
    half = KC // 2
    blocks = [
        jnp.concatenate(
            [turned[k * KC : k * KC + half], turned[k * KC + half : (k + 1) * KC]], axis=1
        )
        for k in range(PN)
    ]
    return jnp.concatenate(blocks, axis=0)


def ghost_kernel(
    send_rows, p_ref, ext_ref, outbox, inbox, own_rows, ghost_rows, send_sem, recv_sem, out_sem
):
    slots = send_rows.shape[0]
    n = p_ref.shape[0]
    barrier = greet()
    for p in ORDER:
        for g in range(slots):
            outbox[p * slots + g] = p_ref[send_rows[g, 0, p]]
    pl.semaphore_wait(barrier, 8)
    copies = {}
    for p in ORDER:
        copies[p] = pltpu.make_async_remote_copy(
            src_ref=outbox.at[pl.ds(p * slots, slots)],
            dst_ref=inbox.at[pl.ds((7 - p) * slots, slots)],
            send_sem=send_sem.at[p],
            recv_sem=recv_sem.at[7 - p],
            device_id=device_at(AROUND[p]),
            device_id_type=MESH,
        )
        copies[p].start()

    def fold_own(r, carry):
        own_rows[r] = folded(p_ref[r])
        return carry

    lax.fori_loop(0, n, fold_own, 0)
    written = [pltpu.make_async_copy(own_rows, ext_ref.at[pl.ds(0, n)], out_sem.at[8])]
    written[0].start()
    for p in reversed(ORDER):
        copies[p].wait_recv()
        first = (7 - p) * slots
        for g in range(slots):
            ghost_rows[first + g] = folded(inbox[first + g])
        written.append(
            pltpu.make_async_copy(
                ghost_rows.at[pl.ds(first, slots)],
                ext_ref.at[pl.ds(n + first, slots)],
                out_sem.at[7 - p],
            )
        )
        written[-1].start()
    for p in ORDER:
        copies[p].wait_send()
    for copy in written:
        copy.wait()


def doubled(chunk, low):
    zero = jnp.zeros_like(chunk)
    left = jnp.where(low, chunk, zero)
    right = jnp.where(low, zero, chunk)
    return left, pltpu.roll(left, KB, 1), pltpu.roll(right, KB, 1), right


def local_kernel(nbr, ap, ts, a_ref, p_ref, x_ref, out_ref, *scratch):
    n = a_ref.shape[0]
    half = KC // 2
    accs = [scratch[2 * u : 2 * u + 2] for u in range(GROUP)]
    part_a, part_b, part_c, part_d = scratch[2 * GROUP :]
    parts = ((part_a, part_b), (part_c, part_d))
    for part in scratch[2 * GROUP :]:
        part[...] = jnp.zeros_like(part)
    low = lax.broadcasted_iota(jnp.int32, (KB, 2 * KB), 1) < KB
    zeros = jnp.zeros((KB, 2 * KB), jnp.bfloat16)

    def apply(e, acc):
        for one in acc:
            one[...] = jnp.zeros_like(one)
        for first in range(0, NB, 2):
            members = [j for j in (first, first + 1) if j < NB]
            if len(members) == 2:
                xx, x1, y0, yy = doubled(a_ref[e, :, first * KB : (first + 2) * KB], low)
                rows = ((xx, zeros), (x1, zeros), (zeros, y0), (zeros, yy))
                weights = jnp.concatenate([jnp.concatenate(row, axis=1) for row in rows], axis=0)
                source = jnp.concatenate([x_ref[nbr[j, e]] for j in members], axis=1)
            else:
                only = jnp.concatenate([a_ref[e, :, first * KB :], zeros[:, :KB]], axis=1)
                weights = jnp.concatenate([only, pltpu.roll(only, KB, 1)], axis=0)
                source = x_ref[nbr[first, e]]
            product = lax.dot_general(
                source, weights, (((1,), (1,)), ((), ())), preferred_element_type=jnp.float32
            )
            for s, j in enumerate(members):
                for k in range(PN):
                    acc[k % 2][ap[j, k, e]] += product[
                        k * half : (k + 1) * half, s * 2 * KB : (s + 1) * 2 * KB
                    ]
        return (acc[0][...] + acc[1][...]).astype(jnp.bfloat16).reshape(QN * half, 2 * KB)

    def project(e, applied):
        xx0, x10, y00, yy0 = doubled(p_ref[e, :, : 2 * KC], low)
        xx1, x11, y01, yy1 = doubled(p_ref[e, :, 2 * KC :], low)
        weights = jnp.concatenate(
            [
                jnp.concatenate([xx0, y00, xx1, y01], axis=1),
                jnp.concatenate([x10, yy0, x11, yy1], axis=1),
            ],
            axis=0,
        )
        contrib = jnp.dot(applied, weights, preferred_element_type=jnp.float32)
        for q in range(QN):
            for k in range(PN):
                parts[k % 2][q % 2][ts[k, q, e]] += contrib[
                    q * half : (q + 1) * half, k * 2 * KC : (k + 1) * 2 * KC
                ]

    def group(i, carry):
        applied = [apply(i * GROUP + u, accs[u]) for u in range(GROUP)]
        for u in range(GROUP):
            project(i * GROUP + u, applied[u])
        return carry

    lax.fori_loop(0, n // GROUP, group, 0)

    def pack(t, carry):
        out_ref[t] = (part_a[t] + part_b[t] + part_c[t] + part_d[t]).astype(jnp.bfloat16)
        return carry

    lax.fori_loop(0, out_ref.shape[0], pack, 0, unroll=8)


def unfolded(first, second):
    rows = [t[:, h * KC : (h + 1) * KC] for t in (first, second) for h in range(2)]
    return jnp.concatenate(rows, axis=0).T


def parcel_kernel(tiles_ref, returned_ref, inbox, send_sem, recv_sem):
    slots = tiles_ref.shape[0] // 9
    barrier = greet()
    pl.semaphore_wait(barrier, 8)
    copies = {}
    for p in ORDER:
        cell = CELLS.index(AROUND[p])
        copies[p] = pltpu.make_async_remote_copy(
            src_ref=tiles_ref.at[pl.ds(cell * slots, slots)],
            dst_ref=inbox.at[pl.ds((8 - cell) * slots, slots)],
            send_sem=send_sem.at[p],
            recv_sem=recv_sem.at[7 - p],
            device_id=device_at(AROUND[p]),
            device_id_type=MESH,
        )
        copies[p].start()

    def settle(source, cell):
        for t in range(cell * slots, (cell + 1) * slots, 2):
            returned_ref[t // 2] = unfolded(source[t], source[t + 1])

    settle(tiles_ref, 4)
    for p in reversed(ORDER):
        copies[p].wait_recv()
        settle(inbox, 8 - CELLS.index(AROUND[p]))
    for p in ORDER:
        copies[p].wait_send()


def owner_kernel(owner_map, returned_ref, out_ref):
    out_ref[...] = jnp.zeros_like(out_ref)
    low = lax.broadcasted_iota(jnp.int32, (KC, 128), 1) < KC

    def add(i, carry):
        pair = returned_ref[i].astype(jnp.float32)
        turned = pltpu.roll(pair, KC, 1)
        for side, same, other in ((0, pair, turned), (1, turned, pair)):
            m = owner_map[0, 2 * i + side]
            at = pl.ds(pl.multiple_of((m // 2) * 128, 128), 128)
            even = lax.rem(m, 2) == 0
            keep = jnp.logical_xor(low, jnp.logical_not(even))
            value = jnp.where(low, same, other)
            out_ref[:, at] += jnp.where(keep, value, 0.0)
        return carry

    lax.fori_loop(0, returned_ref.shape[0], add, 0)


def body(a_strips, p_strips, nbr_local, ap_slot, tile_slot, send_rows, owner_map):
    width = p_strips.shape[2]
    slots = send_rows.shape[2]
    smem = pl.BlockSpec(memory_space=pltpu.SMEM)
    vmem = pl.BlockSpec(memory_space=pltpu.VMEM)
    anywhere = pl.BlockSpec(memory_space=pl.ANY)
    tiles_total = owner_map.shape[1]
    n = a_strips.shape[0]
    folded_rows = pltpu.VMEM((8 * slots, 2 * KC, 2 * KB), jnp.bfloat16)
    raw_rows = pltpu.VMEM((8 * slots, KB, width), jnp.bfloat16)
    extended = pl.pallas_call(
        ghost_kernel,
        out_shape=jax.ShapeDtypeStruct((n + 8 * slots, 2 * KC, 2 * KB), jnp.bfloat16),
        in_specs=[smem, vmem],
        out_specs=anywhere,
        scratch_shapes=[
            raw_rows,
            raw_rows,
            pltpu.VMEM((n, 2 * KC, 2 * KB), jnp.bfloat16),
            folded_rows,
            pltpu.SemaphoreType.DMA((8,)),
            pltpu.SemaphoreType.DMA((8,)),
            pltpu.SemaphoreType.DMA((9,)),
        ],
        compiler_params=pltpu.CompilerParams(collective_id=0, has_side_effects=True),
    )(send_rows.transpose(2, 0, 1), p_strips)
    tiles = pl.pallas_call(
        local_kernel,
        out_shape=jax.ShapeDtypeStruct((tiles_total, KC // 2, 2 * KC), jnp.bfloat16),
        in_specs=[smem, smem, smem, vmem, vmem, vmem],
        out_specs=vmem,
        scratch_shapes=[pltpu.VMEM((QN, KC // 2, 2 * KB), jnp.float32)] * (2 * GROUP)
        + [pltpu.VMEM((tiles_total, KC // 2, 2 * KC), jnp.float32)] * 4,
    )(
        nbr_local.transpose(1, 0),
        ap_slot.transpose(1, 2, 0),
        tile_slot.transpose(1, 2, 0),
        a_strips,
        p_strips,
        extended,
    )
    returned = pl.pallas_call(
        parcel_kernel,
        out_shape=jax.ShapeDtypeStruct((tiles_total // 2, KC, 2 * KC), jnp.bfloat16),
        in_specs=[vmem],
        out_specs=vmem,
        scratch_shapes=[
            pltpu.VMEM(tiles.shape, tiles.dtype),
            pltpu.SemaphoreType.DMA((8,)),
            pltpu.SemaphoreType.DMA((8,)),
        ],
        compiler_params=pltpu.CompilerParams(collective_id=1, has_side_effects=True),
    )(tiles)
    return pl.pallas_call(
        owner_kernel,
        out_shape=jax.ShapeDtypeStruct((KC, OWN * KC), jnp.float32),
        in_specs=[smem, vmem],
        out_specs=vmem,
    )(owner_map, returned)


def solution(mesh):
    placed = (
        P(("dom", "grp"), None, None),
        P(("dom", "grp"), None, None),
        P(("dom", "grp"), None),
        P(("dom", "grp"), None, None),
        P(("dom", "grp"), None, None),
        P(("dom", "grp"), None, None),
        P(("dom", "grp"), None),
    )
    return jax.shard_map(
        body, mesh=mesh, in_specs=placed, out_specs=P(None, ("dom", "grp")), check_vma=False
    )
```

```python
import jax
import jax.numpy as jnp
from jax import lax
from jax.experimental import pallas as pl
from jax.experimental.pallas import tpu as pltpu
from jax.sharding import PartitionSpec as P

KB = 64
KC = 64
NB = 7
PN = 4
QN = 8
OWN = 128
GROUP = 8
MESH = pl.DeviceIdType.MESH
CELLS = [(a, b) for a in (-1, 0, 1) for b in (-1, 0, 1)]
AROUND = [cell for cell in CELLS if cell != (0, 0)]
ORDER = sorted(range(8), key=lambda p: -(abs(AROUND[p][0]) * 2 + abs(AROUND[p][1])))


def device_at(offset):
    rows, cols = lax.axis_size("dom"), lax.axis_size("grp")
    i = lax.rem(lax.axis_index("dom") + offset[0] + rows, rows)
    j = lax.rem(lax.axis_index("grp") + offset[1] + cols, cols)
    return (i, j)


def greet():
    barrier = pltpu.get_barrier_semaphore()
    for offset in AROUND:
        pl.semaphore_signal(barrier, inc=1, device_id=device_at(offset), device_id_type=MESH)
    return barrier


def folded(x):
    turned = x.T
    half = KC // 2
    blocks = [
        jnp.concatenate(
            [turned[k * KC : k * KC + half], turned[k * KC + half : (k + 1) * KC]], axis=1
        )
        for k in range(PN)
    ]
    return jnp.concatenate(blocks, axis=0)


def ghost_kernel(
    send_rows, p_ref, ext_ref, outbox, inbox, own_rows, ghost_rows, send_sem, recv_sem, out_sem
):
    slots = send_rows.shape[0]
    n = p_ref.shape[0]
    barrier = greet()
    for p in ORDER:
        for g in range(slots):
            outbox[p * slots + g] = p_ref[send_rows[g, 0, p]]
    pl.semaphore_wait(barrier, 8)
    copies = {}
    for p in ORDER:
        copies[p] = pltpu.make_async_remote_copy(
            src_ref=outbox.at[pl.ds(p * slots, slots)],
            dst_ref=inbox.at[pl.ds((7 - p) * slots, slots)],
            send_sem=send_sem.at[p],
            recv_sem=recv_sem.at[7 - p],
            device_id=device_at(AROUND[p]),
            device_id_type=MESH,
        )
        copies[p].start()

    def fold_own(r, carry):
        own_rows[r] = folded(p_ref[r])
        return carry

    lax.fori_loop(0, n, fold_own, 0)
    written = [pltpu.make_async_copy(own_rows, ext_ref.at[pl.ds(0, n)], out_sem.at[8])]
    written[0].start()
    for p in reversed(ORDER):
        copies[p].wait_recv()
        first = (7 - p) * slots
        for g in range(slots):
            ghost_rows[first + g] = folded(inbox[first + g])
        written.append(
            pltpu.make_async_copy(
                ghost_rows.at[pl.ds(first, slots)],
                ext_ref.at[pl.ds(n + first, slots)],
                out_sem.at[7 - p],
            )
        )
        written[-1].start()
    for p in ORDER:
        copies[p].wait_send()
    for copy in written:
        copy.wait()


def doubled(chunk, low):
    zero = jnp.zeros_like(chunk)
    left = jnp.where(low, chunk, zero)
    right = jnp.where(low, zero, chunk)
    return left, pltpu.roll(left, KB, 1), pltpu.roll(right, KB, 1), right


def local_kernel(nbr, ap, ts, a_ref, p_ref, x_ref, out_ref, *scratch):
    n = a_ref.shape[0]
    half = KC // 2
    accs = [scratch[2 * u : 2 * u + 2] for u in range(GROUP)]
    part_a, part_b, part_c, part_d = scratch[2 * GROUP :]
    parts = ((part_a, part_b), (part_c, part_d))
    for part in scratch[2 * GROUP :]:
        part[...] = jnp.zeros_like(part)
    low = lax.broadcasted_iota(jnp.int32, (KB, 2 * KB), 1) < KB
    zeros = jnp.zeros((KB, 2 * KB), jnp.bfloat16)

    def apply(e, acc):
        for one in acc:
            one[...] = jnp.zeros_like(one)
        for first in range(0, NB, 2):
            members = [j for j in (first, first + 1) if j < NB]
            if len(members) == 2:
                xx, x1, y0, yy = doubled(a_ref[e, :, first * KB : (first + 2) * KB], low)
                rows = ((xx, zeros), (x1, zeros), (zeros, y0), (zeros, yy))
                weights = jnp.concatenate([jnp.concatenate(row, axis=1) for row in rows], axis=0)
                source = jnp.concatenate([x_ref[nbr[j, e]] for j in members], axis=1)
            else:
                only = jnp.concatenate([a_ref[e, :, first * KB :], zeros[:, :KB]], axis=1)
                weights = jnp.concatenate([only, pltpu.roll(only, KB, 1)], axis=0)
                source = x_ref[nbr[first, e]]
            product = lax.dot_general(
                source, weights, (((1,), (1,)), ((), ())), preferred_element_type=jnp.float32
            )
            for s, j in enumerate(members):
                for k in range(PN):
                    acc[k % 2][ap[j, k, e]] += product[
                        k * half : (k + 1) * half, s * 2 * KB : (s + 1) * 2 * KB
                    ]
        return (acc[0][...] + acc[1][...]).astype(jnp.bfloat16).reshape(QN * half, 2 * KB)

    def project(e, applied):
        xx0, x10, y00, yy0 = doubled(p_ref[e, :, : 2 * KC], low)
        xx1, x11, y01, yy1 = doubled(p_ref[e, :, 2 * KC :], low)
        weights = jnp.concatenate(
            [
                jnp.concatenate([xx0, y00, xx1, y01], axis=1),
                jnp.concatenate([x10, yy0, x11, yy1], axis=1),
            ],
            axis=0,
        )
        contrib = jnp.dot(applied, weights, preferred_element_type=jnp.float32)
        for q in range(QN):
            for k in range(PN):
                parts[k % 2][q % 2][ts[k, q, e]] += contrib[
                    q * half : (q + 1) * half, k * 2 * KC : (k + 1) * 2 * KC
                ]

    def group(i, carry):
        applied = [apply(i * GROUP + u, accs[u]) for u in range(GROUP)]
        for u in range(GROUP):
            project(i * GROUP + u, applied[u])
        return carry

    lax.fori_loop(0, n // GROUP, group, 0)

    def pack(t, carry):
        out_ref[t] = (part_a[t] + part_b[t] + part_c[t] + part_d[t]).astype(jnp.bfloat16)
        return carry

    lax.fori_loop(0, out_ref.shape[0], pack, 0, unroll=8)


def unfolded(first, second):
    rows = [t[:, h * KC : (h + 1) * KC] for t in (first, second) for h in range(2)]
    return jnp.concatenate(rows, axis=0).T


def parcel_kernel(tiles_ref, returned_ref, inbox, send_sem, recv_sem):
    slots = tiles_ref.shape[0] // 9
    barrier = greet()
    pl.semaphore_wait(barrier, 8)
    copies = {}
    for p in ORDER:
        cell = CELLS.index(AROUND[p])
        copies[p] = pltpu.make_async_remote_copy(
            src_ref=tiles_ref.at[pl.ds(cell * slots, slots)],
            dst_ref=inbox.at[pl.ds((8 - cell) * slots, slots)],
            send_sem=send_sem.at[p],
            recv_sem=recv_sem.at[7 - p],
            device_id=device_at(AROUND[p]),
            device_id_type=MESH,
        )
        copies[p].start()

    def settle(source, cell):
        for t in range(cell * slots, (cell + 1) * slots, 2):
            returned_ref[t // 2] = unfolded(source[t], source[t + 1])

    settle(tiles_ref, 4)
    for p in reversed(ORDER):
        copies[p].wait_recv()
        settle(inbox, 8 - CELLS.index(AROUND[p]))
    for p in ORDER:
        copies[p].wait_send()


def owner_kernel(owner_map, returned_ref, out_ref):
    out_ref[...] = jnp.zeros_like(out_ref)
    low = lax.broadcasted_iota(jnp.int32, (KC, 128), 1) < KC

    def add(i, carry):
        pair = returned_ref[i].astype(jnp.float32)
        turned = pltpu.roll(pair, KC, 1)
        for side, same, other in ((0, pair, turned), (1, turned, pair)):
            m = owner_map[0, 2 * i + side]
            at = pl.ds(pl.multiple_of((m // 2) * 128, 128), 128)
            even = lax.rem(m, 2) == 0
            keep = jnp.logical_xor(low, jnp.logical_not(even))
            value = jnp.where(low, same, other)
            out_ref[:, at] += jnp.where(keep, value, 0.0)
        return carry

    lax.fori_loop(0, returned_ref.shape[0], add, 0)


def body(a_strips, p_strips, nbr_local, ap_slot, tile_slot, send_rows, owner_map):
    width = p_strips.shape[2]
    slots = send_rows.shape[2]
    smem = pl.BlockSpec(memory_space=pltpu.SMEM)
    vmem = pl.BlockSpec(memory_space=pltpu.VMEM)
    anywhere = pl.BlockSpec(memory_space=pl.ANY)
    tiles_total = owner_map.shape[1]
    n = a_strips.shape[0]
    folded_rows = pltpu.VMEM((8 * slots, 2 * KC, 2 * KB), jnp.bfloat16)
    raw_rows = pltpu.VMEM((8 * slots, KB, width), jnp.bfloat16)
    extended = pl.pallas_call(
        ghost_kernel,
        out_shape=jax.ShapeDtypeStruct((n + 8 * slots, 2 * KC, 2 * KB), jnp.bfloat16),
        in_specs=[smem, vmem],
        out_specs=anywhere,
        scratch_shapes=[
            raw_rows,
            raw_rows,
            pltpu.VMEM((n, 2 * KC, 2 * KB), jnp.bfloat16),
            folded_rows,
            pltpu.SemaphoreType.DMA((8,)),
            pltpu.SemaphoreType.DMA((8,)),
            pltpu.SemaphoreType.DMA((9,)),
        ],
        compiler_params=pltpu.CompilerParams(collective_id=0, has_side_effects=True, vmem_limit_bytes=12 << 20),
    )(send_rows.transpose(2, 0, 1), p_strips)
    tiles = pl.pallas_call(
        local_kernel,
        out_shape=jax.ShapeDtypeStruct((tiles_total, KC // 2, 2 * KC), jnp.bfloat16),
        in_specs=[smem, smem, smem, vmem, vmem, vmem],
        out_specs=vmem,
        scratch_shapes=[pltpu.VMEM((QN, KC // 2, 2 * KB), jnp.float32)] * (2 * GROUP)
        + [pltpu.VMEM((tiles_total, KC // 2, 2 * KC), jnp.float32)] * 4,
        compiler_params=pltpu.CompilerParams(vmem_limit_bytes=20 << 20),
    )(
        nbr_local.transpose(1, 0),
        ap_slot.transpose(1, 2, 0),
        tile_slot.transpose(1, 2, 0),
        a_strips,
        p_strips,
        extended,
    )
    returned = pl.pallas_call(
        parcel_kernel,
        out_shape=jax.ShapeDtypeStruct((tiles_total // 2, KC, 2 * KC), jnp.bfloat16),
        in_specs=[vmem],
        out_specs=vmem,
        scratch_shapes=[
            pltpu.VMEM(tiles.shape, tiles.dtype),
            pltpu.SemaphoreType.DMA((8,)),
            pltpu.SemaphoreType.DMA((8,)),
        ],
        compiler_params=pltpu.CompilerParams(collective_id=1, has_side_effects=True, vmem_limit_bytes=8 << 20),
    )(tiles)
    return pl.pallas_call(
        owner_kernel,
        out_shape=jax.ShapeDtypeStruct((KC, OWN * KC), jnp.float32),
        in_specs=[smem, vmem],
        out_specs=vmem,
        compiler_params=pltpu.CompilerParams(vmem_limit_bytes=8 << 20),
    )(owner_map, returned)


def solution(mesh):
    placed = (
        P(("dom", "grp"), None, None),
        P(("dom", "grp"), None, None),
        P(("dom", "grp"), None),
        P(("dom", "grp"), None, None),
        P(("dom", "grp"), None, None),
        P(("dom", "grp"), None, None),
        P(("dom", "grp"), None),
    )
    return jax.shard_map(
        body, mesh=mesh, in_specs=placed, out_specs=P(None, ("dom", "grp")), check_vma=False
    )
```

```python
import jax
import jax.numpy as jnp
from jax import lax
from jax.experimental import pallas as pl
from jax.experimental.pallas import tpu as pltpu
from jax.sharding import PartitionSpec as P

KB = 64
KC = 64
NB = 7
PN = 4
QN = 8
OWN = 128
GROUP = 8
MESH = pl.DeviceIdType.MESH
CELLS = [(a, b) for a in (-1, 0, 1) for b in (-1, 0, 1)]
AROUND = [cell for cell in CELLS if cell != (0, 0)]
ORDER = sorted(range(8), key=lambda p: -(abs(AROUND[p][0]) * 2 + abs(AROUND[p][1])))


def device_at(offset):
    rows, cols = lax.axis_size("dom"), lax.axis_size("grp")
    i = lax.rem(lax.axis_index("dom") + offset[0] + rows, rows)
    j = lax.rem(lax.axis_index("grp") + offset[1] + cols, cols)
    return (i, j)


def greet():
    barrier = pltpu.get_barrier_semaphore()
    for offset in AROUND:
        pl.semaphore_signal(barrier, inc=1, device_id=device_at(offset), device_id_type=MESH)
    return barrier


def folded(x):
    turned = x.T
    half = KC // 2
    blocks = [
        jnp.concatenate(
            [turned[k * KC : k * KC + half], turned[k * KC + half : (k + 1) * KC]], axis=1
        )
        for k in range(PN)
    ]
    return jnp.concatenate(blocks, axis=0)


def ghost_kernel(
    rows_hbm, p_hbm, ext_ref, send_rows, own_rows, outbox, inbox, send_sem, recv_sem, load_sem
):
    slots = rows_hbm.shape[0]
    n = p_hbm.shape[0]
    loads = (
        pltpu.make_async_copy(rows_hbm, send_rows, load_sem.at[0]),
        pltpu.make_async_copy(p_hbm, own_rows, load_sem.at[1]),
    )
    for load in loads:
        load.start()
    barrier = greet()
    for load in loads:
        load.wait()

    def fill(p):
        for g in range(slots):
            outbox[p * slots + g] = own_rows[send_rows[g, 0, p]]

    copies = {}
    for p in ORDER:
        copies[p] = pltpu.make_async_remote_copy(
            src_ref=outbox.at[pl.ds(p * slots, slots)],
            dst_ref=inbox.at[pl.ds((7 - p) * slots, slots)],
            send_sem=send_sem.at[p],
            recv_sem=recv_sem.at[7 - p],
            device_id=device_at(AROUND[p]),
            device_id_type=MESH,
        )
    fill(ORDER[0])
    fill(ORDER[1])
    pl.semaphore_wait(barrier, 8)
    for at, p in enumerate(ORDER):
        copies[p].start()
        if at + 2 < len(ORDER):
            fill(ORDER[at + 2])

    def fold_own(r, carry):
        ext_ref[r] = folded(own_rows[r])
        return carry

    lax.fori_loop(0, n, fold_own, 0)
    for p in reversed(ORDER):
        copies[p].wait_recv()
        for g in range((7 - p) * slots, (8 - p) * slots):
            ext_ref[n + g] = folded(inbox[g])
    for p in ORDER:
        copies[p].wait_send()


def doubled(chunk, low):
    zero = jnp.zeros_like(chunk)
    left = jnp.where(low, chunk, zero)
    right = jnp.where(low, zero, chunk)
    return left, pltpu.roll(left, KB, 1), pltpu.roll(right, KB, 1), right


def local_kernel(nbr, ap, ts, a_ref, p_ref, x_ref, out_ref, *scratch):
    n = a_ref.shape[0]
    half = KC // 2
    accs = [scratch[2 * u : 2 * u + 2] for u in range(GROUP)]
    part_a, part_b, part_c, part_d = scratch[2 * GROUP :]
    parts = ((part_a, part_b), (part_c, part_d))
    for part in scratch[2 * GROUP :]:
        part[...] = jnp.zeros_like(part)
    low = lax.broadcasted_iota(jnp.int32, (KB, 2 * KB), 1) < KB
    zeros = jnp.zeros((KB, 2 * KB), jnp.bfloat16)

    def apply(e, acc):
        for one in acc:
            one[...] = jnp.zeros_like(one)
        for first in range(0, NB, 2):
            members = [j for j in (first, first + 1) if j < NB]
            if len(members) == 2:
                xx, x1, y0, yy = doubled(a_ref[e, :, first * KB : (first + 2) * KB], low)
                rows = ((xx, zeros), (x1, zeros), (zeros, y0), (zeros, yy))
                weights = jnp.concatenate([jnp.concatenate(row, axis=1) for row in rows], axis=0)
                source = jnp.concatenate([x_ref[nbr[j, e]] for j in members], axis=1)
            else:
                only = jnp.concatenate([a_ref[e, :, first * KB :], zeros[:, :KB]], axis=1)
                weights = jnp.concatenate([only, pltpu.roll(only, KB, 1)], axis=0)
                source = x_ref[nbr[first, e]]
            product = lax.dot_general(
                source, weights, (((1,), (1,)), ((), ())), preferred_element_type=jnp.float32
            )
            for s, j in enumerate(members):
                for k in range(PN):
                    acc[k % 2][ap[j, k, e]] += product[
                        k * half : (k + 1) * half, s * 2 * KB : (s + 1) * 2 * KB
                    ]
        return (acc[0][...] + acc[1][...]).astype(jnp.bfloat16).reshape(QN * half, 2 * KB)

    def project(e, applied):
        xx0, x10, y00, yy0 = doubled(p_ref[e, :, : 2 * KC], low)
        xx1, x11, y01, yy1 = doubled(p_ref[e, :, 2 * KC :], low)
        weights = jnp.concatenate(
            [
                jnp.concatenate([xx0, y00, xx1, y01], axis=1),
                jnp.concatenate([x10, yy0, x11, yy1], axis=1),
            ],
            axis=0,
        )
        contrib = jnp.dot(applied, weights, preferred_element_type=jnp.float32)
        for q in range(QN):
            for k in range(PN):
                parts[k % 2][q % 2][ts[k, q, e]] += contrib[
                    q * half : (q + 1) * half, k * 2 * KC : (k + 1) * 2 * KC
                ]

    def group(i, carry):
        applied = [apply(i * GROUP + u, accs[u]) for u in range(GROUP)]
        for u in range(GROUP):
            project(i * GROUP + u, applied[u])
        return carry

    lax.fori_loop(0, n // GROUP, group, 0)

    def pack(t, carry):
        out_ref[t] = (part_a[t] + part_b[t] + part_c[t] + part_d[t]).astype(jnp.bfloat16)
        return carry

    lax.fori_loop(0, out_ref.shape[0], pack, 0, unroll=8)


def unfolded(first, second):
    rows = [t[:, h * KC : (h + 1) * KC] for t in (first, second) for h in range(2)]
    return jnp.concatenate(rows, axis=0).T


def parcel_kernel(tiles_ref, returned_ref, inbox, send_sem, recv_sem):
    slots = tiles_ref.shape[0] // 9
    barrier = greet()
    pl.semaphore_wait(barrier, 8)
    copies = {}
    for p in ORDER:
        cell = CELLS.index(AROUND[p])
        copies[p] = pltpu.make_async_remote_copy(
            src_ref=tiles_ref.at[pl.ds(cell * slots, slots)],
            dst_ref=inbox.at[pl.ds((8 - cell) * slots, slots)],
            send_sem=send_sem.at[p],
            recv_sem=recv_sem.at[7 - p],
            device_id=device_at(AROUND[p]),
            device_id_type=MESH,
        )
        copies[p].start()

    def settle(source, cell):
        for t in range(cell * slots, (cell + 1) * slots, 2):
            returned_ref[t // 2] = unfolded(source[t], source[t + 1])

    settle(tiles_ref, 4)
    for p in reversed(ORDER):
        copies[p].wait_recv()
        settle(inbox, 8 - CELLS.index(AROUND[p]))
    for p in ORDER:
        copies[p].wait_send()


def owner_kernel(owner_map, returned_ref, out_ref):
    out_ref[...] = jnp.zeros_like(out_ref)
    low = lax.broadcasted_iota(jnp.int32, (KC, 128), 1) < KC

    def add(i, carry):
        pair = returned_ref[i].astype(jnp.float32)
        turned = pltpu.roll(pair, KC, 1)
        for side, same, other in ((0, pair, turned), (1, turned, pair)):
            m = owner_map[0, 2 * i + side]
            at = pl.ds(pl.multiple_of((m // 2) * 128, 128), 128)
            even = lax.rem(m, 2) == 0
            keep = jnp.logical_xor(low, jnp.logical_not(even))
            value = jnp.where(low, same, other)
            out_ref[:, at] += jnp.where(keep, value, 0.0)
        return carry

    lax.fori_loop(0, returned_ref.shape[0], add, 0)


def body(a_strips, p_strips, nbr_local, ap_slot, tile_slot, send_rows, owner_map):
    width = p_strips.shape[2]
    slots = send_rows.shape[2]
    smem = pl.BlockSpec(memory_space=pltpu.SMEM)
    vmem = pl.BlockSpec(memory_space=pltpu.VMEM)
    tiles_total = owner_map.shape[1]
    n = a_strips.shape[0]
    extended = pl.pallas_call(
        ghost_kernel,
        out_shape=jax.ShapeDtypeStruct((n + 8 * slots, 2 * KC, 2 * KB), jnp.bfloat16),
        in_specs=[pl.BlockSpec(memory_space=pltpu.HBM)] * 2,
        out_specs=vmem,
        scratch_shapes=[
            pltpu.SMEM((slots, 1, 8), jnp.int32),
            pltpu.VMEM((n, KB, width), jnp.bfloat16),
            pltpu.VMEM((8 * slots, KB, width), jnp.bfloat16),
            pltpu.VMEM((8 * slots, KB, width), jnp.bfloat16),
            pltpu.SemaphoreType.DMA((8,)),
            pltpu.SemaphoreType.DMA((8,)),
            pltpu.SemaphoreType.DMA((2,)),
        ],
        compiler_params=pltpu.CompilerParams(collective_id=0, has_side_effects=True, vmem_limit_bytes=12 << 20),
    )(
        pltpu.with_memory_space_constraint(send_rows.transpose(2, 0, 1), pltpu.HBM),
        pltpu.with_memory_space_constraint(p_strips, pltpu.HBM),
    )
    tiles = pl.pallas_call(
        local_kernel,
        out_shape=jax.ShapeDtypeStruct((tiles_total, KC // 2, 2 * KC), jnp.bfloat16),
        in_specs=[smem, smem, smem, vmem, vmem, vmem],
        out_specs=vmem,
        scratch_shapes=[pltpu.VMEM((QN, KC // 2, 2 * KB), jnp.float32)] * (2 * GROUP)
        + [pltpu.VMEM((tiles_total, KC // 2, 2 * KC), jnp.float32)] * 4,
        compiler_params=pltpu.CompilerParams(
            vmem_limit_bytes=20 << 20
        ),
    )(
        nbr_local.transpose(1, 0),
        ap_slot.transpose(1, 2, 0),
        tile_slot.transpose(1, 2, 0),
        a_strips,
        p_strips,
        extended,
    )
    returned = pl.pallas_call(
        parcel_kernel,
        out_shape=jax.ShapeDtypeStruct((tiles_total // 2, KC, 2 * KC), jnp.bfloat16),
        in_specs=[vmem],
        out_specs=vmem,
        scratch_shapes=[
            pltpu.VMEM(tiles.shape, tiles.dtype),
            pltpu.SemaphoreType.DMA((8,)),
            pltpu.SemaphoreType.DMA((8,)),
        ],
        compiler_params=pltpu.CompilerParams(collective_id=1, has_side_effects=True, vmem_limit_bytes=8 << 20),
    )(tiles)
    return pl.pallas_call(
        owner_kernel,
        out_shape=jax.ShapeDtypeStruct((KC, OWN * KC), jnp.float32),
        in_specs=[smem, vmem],
        out_specs=vmem,
        compiler_params=pltpu.CompilerParams(vmem_limit_bytes=8 << 20),
    )(owner_map, returned)


def solution(mesh):
    placed = (
        P(("dom", "grp"), None, None),
        P(("dom", "grp"), None, None),
        P(("dom", "grp"), None),
        P(("dom", "grp"), None, None),
        P(("dom", "grp"), None, None),
        P(("dom", "grp"), None, None),
        P(("dom", "grp"), None),
    )
    return jax.shard_map(
        body, mesh=mesh, in_specs=placed, out_specs=P(None, ("dom", "grp")), check_vma=False
    )
```

```python
import jax
import jax.numpy as jnp
from jax import lax
from jax.experimental import pallas as pl
from jax.experimental.pallas import tpu as pltpu
from jax.sharding import PartitionSpec as P

KB = 64
KC = 64
NB = 7
PN = 4
QN = 8
OWN = 128
GROUP = 8
MESH = pl.DeviceIdType.MESH
CELLS = [(a, b) for a in (-1, 0, 1) for b in (-1, 0, 1)]
AROUND = [cell for cell in CELLS if cell != (0, 0)]
ORDER = sorted(range(8), key=lambda p: -(abs(AROUND[p][0]) * 2 + abs(AROUND[p][1])))


def device_at(offset):
    rows, cols = lax.axis_size("dom"), lax.axis_size("grp")
    i = lax.rem(lax.axis_index("dom") + offset[0] + rows, rows)
    j = lax.rem(lax.axis_index("grp") + offset[1] + cols, cols)
    return (i, j)


def greet():
    barrier = pltpu.get_barrier_semaphore()
    for offset in AROUND:
        pl.semaphore_signal(barrier, inc=1, device_id=device_at(offset), device_id_type=MESH)
    return barrier


def folded(x):
    turned = x.T
    half = KC // 2
    blocks = [
        jnp.concatenate(
            [turned[k * KC : k * KC + half], turned[k * KC + half : (k + 1) * KC]], axis=1
        )
        for k in range(PN)
    ]
    return jnp.concatenate(blocks, axis=0)


def doubled(chunk, low):
    zero = jnp.zeros_like(chunk)
    left = jnp.where(low, chunk, zero)
    right = jnp.where(low, zero, chunk)
    return left, pltpu.roll(left, KB, 1), pltpu.roll(right, KB, 1), right


def ghost_kernel(
    rows_hbm,
    p_hbm,
    a_hbm,
    ext_ref,
    weights_ref,
    send_rows,
    own_rows,
    operator,
    outbox,
    inbox,
    send_sem,
    recv_sem,
    load_sem,
):
    slots = rows_hbm.shape[0]
    n = p_hbm.shape[0]
    loads = (
        pltpu.make_async_copy(rows_hbm, send_rows, load_sem.at[0]),
        pltpu.make_async_copy(p_hbm, own_rows, load_sem.at[1]),
        pltpu.make_async_copy(a_hbm, operator, load_sem.at[2]),
    )
    for load in loads:
        load.start()
    barrier = greet()
    for load in loads[:2]:
        load.wait()

    def fill(p):
        for g in range(slots):
            outbox[p * slots + g] = own_rows[send_rows[g, 0, p]]

    copies = {}
    for p in ORDER:
        copies[p] = pltpu.make_async_remote_copy(
            src_ref=outbox.at[pl.ds(p * slots, slots)],
            dst_ref=inbox.at[pl.ds((7 - p) * slots, slots)],
            send_sem=send_sem.at[p],
            recv_sem=recv_sem.at[7 - p],
            device_id=device_at(AROUND[p]),
            device_id_type=MESH,
        )
    fill(ORDER[0])
    fill(ORDER[1])
    pl.semaphore_wait(barrier, 8)
    for at, p in enumerate(ORDER):
        copies[p].start()
        if at + 2 < len(ORDER):
            fill(ORDER[at + 2])

    def fold_own(r, carry):
        ext_ref[r] = folded(own_rows[r])
        return carry

    lax.fori_loop(0, n, fold_own, 0)
    loads[2].wait()
    low = lax.broadcasted_iota(jnp.int32, (KB, 2 * KB), 1) < KB

    def spread(e, carry):
        turned = operator[e].T
        for pair in range((NB + 1) // 2):
            left = turned[2 * pair * KB : (2 * pair + 1) * KB]
            if 2 * pair + 1 < NB:
                right = turned[(2 * pair + 1) * KB : (2 * pair + 2) * KB]
            else:
                right = jnp.zeros_like(left)
            for v, piece in enumerate(doubled(jnp.concatenate([left, right], axis=1), low)):
                weights_ref[e, pair, v] = piece
        return carry

    lax.fori_loop(0, n, spread, 0)
    for p in reversed(ORDER):
        copies[p].wait_recv()
        for g in range((7 - p) * slots, (8 - p) * slots):
            ext_ref[n + g] = folded(inbox[g])
    for p in ORDER:
        copies[p].wait_send()


def local_kernel(nbr, ap, ts, a_ref, p_ref, x_ref, out_ref, *scratch):
    n = a_ref.shape[0]
    half = KC // 2
    accs = [scratch[2 * u : 2 * u + 2] for u in range(GROUP)]
    part_a, part_b, part_c, part_d = scratch[2 * GROUP :]
    parts = ((part_a, part_b), (part_c, part_d))
    for part in scratch[2 * GROUP :]:
        part[...] = jnp.zeros_like(part)
    low = lax.broadcasted_iota(jnp.int32, (KB, 2 * KB), 1) < KB
    zeros = jnp.zeros((KB, 2 * KB), jnp.bfloat16)

    def apply(e, acc):
        for one in acc:
            one[...] = jnp.zeros_like(one)
        for first in range(0, NB, 2):
            members = [j for j in (first, first + 1) if j < NB]
            pieces = [a_ref[e, first // 2, v] for v in range(2 * len(members))]
            if len(members) == 2:
                rows = (
                    (pieces[0], zeros),
                    (pieces[1], zeros),
                    (zeros, pieces[2]),
                    (zeros, pieces[3]),
                )
                weights = jnp.concatenate([jnp.concatenate(row, axis=1) for row in rows], axis=0)
            else:
                weights = jnp.concatenate(pieces, axis=0)
            source = jnp.concatenate([x_ref[nbr[j, e]] for j in members], axis=1)
            product = jnp.dot(source, weights, preferred_element_type=jnp.float32)
            for s, j in enumerate(members):
                for k in range(PN):
                    acc[k % 2][ap[j, k, e]] += product[
                        k * half : (k + 1) * half, s * 2 * KB : (s + 1) * 2 * KB
                    ]
        return (acc[0][...] + acc[1][...]).astype(jnp.bfloat16).reshape(QN * half, 2 * KB)

    def project(e, applied):
        xx0, x10, y00, yy0 = doubled(p_ref[e, :, : 2 * KC], low)
        xx1, x11, y01, yy1 = doubled(p_ref[e, :, 2 * KC :], low)
        weights = jnp.concatenate(
            [
                jnp.concatenate([xx0, y00, xx1, y01], axis=1),
                jnp.concatenate([x10, yy0, x11, yy1], axis=1),
            ],
            axis=0,
        )
        contrib = jnp.dot(applied, weights, preferred_element_type=jnp.float32)
        for q in range(QN):
            for k in range(PN):
                parts[k % 2][q % 2][ts[k, q, e]] += contrib[
                    q * half : (q + 1) * half, k * 2 * KC : (k + 1) * 2 * KC
                ]

    def group(i, carry):
        applied = [apply(i * GROUP + u, accs[u]) for u in range(GROUP)]
        for u in range(GROUP):
            project(i * GROUP + u, applied[u])
        return carry

    lax.fori_loop(0, n // GROUP, group, 0)

    def pack(t, carry):
        out_ref[t] = (part_a[t] + part_b[t] + part_c[t] + part_d[t]).astype(jnp.bfloat16)
        return carry

    lax.fori_loop(0, out_ref.shape[0], pack, 0, unroll=8)


def unfolded(first, second):
    rows = [t[:, h * KC : (h + 1) * KC] for t in (first, second) for h in range(2)]
    return jnp.concatenate(rows, axis=0).T


def parcel_kernel(tiles_ref, returned_ref, inbox, send_sem, recv_sem):
    slots = tiles_ref.shape[0] // 9
    barrier = greet()
    pl.semaphore_wait(barrier, 8)
    copies = {}
    for p in ORDER:
        cell = CELLS.index(AROUND[p])
        copies[p] = pltpu.make_async_remote_copy(
            src_ref=tiles_ref.at[pl.ds(cell * slots, slots)],
            dst_ref=inbox.at[pl.ds((8 - cell) * slots, slots)],
            send_sem=send_sem.at[p],
            recv_sem=recv_sem.at[7 - p],
            device_id=device_at(AROUND[p]),
            device_id_type=MESH,
        )
        copies[p].start()

    def settle(source, cell):
        for t in range(cell * slots, (cell + 1) * slots, 2):
            returned_ref[t // 2] = unfolded(source[t], source[t + 1])

    settle(tiles_ref, 4)
    for p in reversed(ORDER):
        copies[p].wait_recv()
        settle(inbox, 8 - CELLS.index(AROUND[p]))
    for p in ORDER:
        copies[p].wait_send()


def owner_kernel(owner_map, returned_ref, out_ref):
    out_ref[...] = jnp.zeros_like(out_ref)
    low = lax.broadcasted_iota(jnp.int32, (KC, 2 * KC), 1) < KC
    right = 1 - low.astype(jnp.int32)
    for t in range(returned_ref.shape[0]):
        pair = returned_ref[t].astype(jnp.float32)
        turned = pltpu.roll(pair, KC, 1)
        both = (jnp.where(low, pair, turned), jnp.where(low, turned, pair))
        for side, tile in enumerate(both):
            m = owner_map[0, 2 * t + side]
            at = pl.ds(pl.multiple_of(lax.shift_right_logical(m, 1) * 2 * KC, 2 * KC), 2 * KC)
            out_ref[:, at] += jnp.where(right == jnp.bitwise_and(m, 1), tile, 0.0)


def body(a_strips, p_strips, nbr_local, ap_slot, tile_slot, send_rows, owner_map):
    width = p_strips.shape[2]
    slots = send_rows.shape[2]
    smem = pl.BlockSpec(memory_space=pltpu.SMEM)
    vmem = pl.BlockSpec(memory_space=pltpu.VMEM)
    tiles_total = owner_map.shape[1]
    n = a_strips.shape[0]
    extended, weights = pl.pallas_call(
        ghost_kernel,
        out_shape=(
            jax.ShapeDtypeStruct((n + 8 * slots, 2 * KC, 2 * KB), jnp.bfloat16),
            jax.ShapeDtypeStruct((n, (NB + 1) // 2, 4, KB, 2 * KB), jnp.bfloat16),
        ),
        in_specs=[pl.BlockSpec(memory_space=pltpu.HBM)] * 3,
        out_specs=(vmem, vmem),
        scratch_shapes=[
            pltpu.SMEM((slots, 1, 8), jnp.int32),
            pltpu.VMEM((n, KB, width), jnp.bfloat16),
            pltpu.VMEM(a_strips.shape, a_strips.dtype),
            pltpu.VMEM((8 * slots, KB, width), jnp.bfloat16),
            pltpu.VMEM((8 * slots, KB, width), jnp.bfloat16),
            pltpu.SemaphoreType.DMA((8,)),
            pltpu.SemaphoreType.DMA((8,)),
            pltpu.SemaphoreType.DMA((3,)),
        ],
        compiler_params=pltpu.CompilerParams(collective_id=0, has_side_effects=True, vmem_limit_bytes=24 << 20),
    )(
        pltpu.with_memory_space_constraint(send_rows.transpose(2, 0, 1), pltpu.HBM),
        pltpu.with_memory_space_constraint(p_strips, pltpu.HBM),
        pltpu.with_memory_space_constraint(a_strips, pltpu.HBM),
    )
    tiles = pl.pallas_call(
        local_kernel,
        out_shape=jax.ShapeDtypeStruct((tiles_total, KC // 2, 2 * KC), jnp.bfloat16),
        in_specs=[smem, smem, smem, vmem, vmem, vmem],
        out_specs=vmem,
        scratch_shapes=[pltpu.VMEM((QN, KC // 2, 2 * KB), jnp.float32)] * (2 * GROUP)
        + [pltpu.VMEM((tiles_total, KC // 2, 2 * KC), jnp.float32)] * 4,
        compiler_params=pltpu.CompilerParams(
            vmem_limit_bytes=20 << 20
        ),
    )(
        nbr_local.transpose(1, 0),
        ap_slot.transpose(1, 2, 0),
        tile_slot.transpose(1, 2, 0),
        weights,
        p_strips,
        extended,
    )
    returned = pl.pallas_call(
        parcel_kernel,
        out_shape=jax.ShapeDtypeStruct((tiles_total // 2, KC, 2 * KC), jnp.bfloat16),
        in_specs=[vmem],
        out_specs=vmem,
        scratch_shapes=[
            pltpu.VMEM(tiles.shape, tiles.dtype),
            pltpu.SemaphoreType.DMA((8,)),
            pltpu.SemaphoreType.DMA((8,)),
        ],
        compiler_params=pltpu.CompilerParams(collective_id=1, has_side_effects=True, vmem_limit_bytes=8 << 20),
    )(tiles)
    return pl.pallas_call(
        owner_kernel,
        out_shape=jax.ShapeDtypeStruct((KC, OWN * KC), jnp.float32),
        in_specs=[smem, vmem],
        out_specs=vmem,
        compiler_params=pltpu.CompilerParams(vmem_limit_bytes=8 << 20),
    )(owner_map, returned)


def solution(mesh):
    placed = (
        P(("dom", "grp"), None, None),
        P(("dom", "grp"), None, None),
        P(("dom", "grp"), None),
        P(("dom", "grp"), None, None),
        P(("dom", "grp"), None, None),
        P(("dom", "grp"), None, None),
        P(("dom", "grp"), None),
    )
    return jax.shard_map(
        body, mesh=mesh, in_specs=placed, out_specs=P(None, ("dom", "grp")), check_vma=False
    )
```

```python
import jax
import jax.numpy as jnp
from jax import lax
from jax.experimental import pallas as pl
from jax.experimental.pallas import tpu as pltpu
from jax.sharding import PartitionSpec as P

KB = 64
KC = 64
NB = 7
PN = 4
QN = 8
OWN = 128
GROUP = 8
MESH = pl.DeviceIdType.MESH
CELLS = [(a, b) for a in (-1, 0, 1) for b in (-1, 0, 1)]
AROUND = [cell for cell in CELLS if cell != (0, 0)]
ORDER = sorted(range(8), key=lambda p: -(abs(AROUND[p][0]) * 2 + abs(AROUND[p][1])))


def device_at(offset):
    rows, cols = lax.axis_size("dom"), lax.axis_size("grp")
    i = lax.rem(lax.axis_index("dom") + offset[0] + rows, rows)
    j = lax.rem(lax.axis_index("grp") + offset[1] + cols, cols)
    return (i, j)


def greet():
    barrier = pltpu.get_barrier_semaphore()
    for offset in AROUND:
        pl.semaphore_signal(barrier, inc=1, device_id=device_at(offset), device_id_type=MESH)
    return barrier


def folded(x):
    turned = x.T
    half = KC // 2
    blocks = [
        jnp.concatenate(
            [turned[k * KC : k * KC + half], turned[k * KC + half : (k + 1) * KC]], axis=1
        )
        for k in range(PN)
    ]
    return jnp.concatenate(blocks, axis=0)


def doubled(chunk, low):
    zero = jnp.zeros_like(chunk)
    left = jnp.where(low, chunk, zero)
    right = jnp.where(low, zero, chunk)
    return left, pltpu.roll(left, KB, 1), pltpu.roll(right, KB, 1), right


def ghost_kernel(
    rows_hbm,
    p_hbm,
    a_hbm,
    ext_ref,
    weights_ref,
    own_rows,
    send_rows,
    operator,
    outbox,
    inbox,
    send_sem,
    recv_sem,
    load_sem,
):
    slots = rows_hbm.shape[0]
    n = p_hbm.shape[0]
    loads = (
        pltpu.make_async_copy(rows_hbm, send_rows, load_sem.at[0]),
        pltpu.make_async_copy(p_hbm, own_rows, load_sem.at[1]),
        pltpu.make_async_copy(a_hbm, operator, load_sem.at[2]),
    )
    for load in loads[:2]:
        load.start()
    barrier = greet()
    for load in loads[:2]:
        load.wait()

    def fill(p):
        for g in range(slots):
            outbox[p * slots + g] = own_rows[send_rows[g, 0, p]]

    copies = {}
    for p in ORDER:
        copies[p] = pltpu.make_async_remote_copy(
            src_ref=outbox.at[pl.ds(p * slots, slots)],
            dst_ref=inbox.at[pl.ds((7 - p) * slots, slots)],
            send_sem=send_sem.at[p],
            recv_sem=recv_sem.at[7 - p],
            device_id=device_at(AROUND[p]),
            device_id_type=MESH,
        )
    fill(ORDER[0])
    fill(ORDER[1])
    pl.semaphore_wait(barrier, 8)
    for at, p in enumerate(ORDER):
        copies[p].start()
        if at + 2 < len(ORDER):
            fill(ORDER[at + 2])
    loads[2].start()

    def fold_own(r, carry):
        ext_ref[r] = folded(own_rows[r])
        return carry

    lax.fori_loop(0, n, fold_own, 0)
    loads[2].wait()
    low = lax.broadcasted_iota(jnp.int32, (KB, 2 * KB), 1) < KB

    def spread(e, carry):
        turned = operator[e].T
        for pair in range((NB + 1) // 2):
            left = turned[2 * pair * KB : (2 * pair + 1) * KB]
            if 2 * pair + 1 < NB:
                right = turned[(2 * pair + 1) * KB : (2 * pair + 2) * KB]
            else:
                right = jnp.zeros_like(left)
            for v, piece in enumerate(doubled(jnp.concatenate([left, right], axis=1), low)):
                weights_ref[e, pair, v] = piece
        return carry

    lax.fori_loop(0, n, spread, 0)
    for p in reversed(ORDER):
        copies[p].wait_recv()
        for g in range((7 - p) * slots, (8 - p) * slots):
            ext_ref[n + g] = folded(inbox[g])
    for p in ORDER:
        copies[p].wait_send()


def local_kernel(nbr, ap, ts, a_ref, p_ref, x_ref, out_ref, *scratch):
    n = a_ref.shape[0]
    half = KC // 2
    accs = [scratch[2 * u : 2 * u + 2] for u in range(GROUP)]
    part_a, part_b, part_c, part_d = scratch[2 * GROUP :]
    parts = ((part_a, part_b), (part_c, part_d))
    low = lax.broadcasted_iota(jnp.int32, (KB, 2 * KB), 1) < KB
    zeros = jnp.zeros((KB, 2 * KB), jnp.bfloat16)

    def apply(e, acc):
        for first in range(0, NB, 2):
            members = [j for j in (first, first + 1) if j < NB]
            pieces = [a_ref[e, first // 2, v] for v in range(2 * len(members))]
            if len(members) == 2:
                rows = (
                    (pieces[0], zeros),
                    (pieces[1], zeros),
                    (zeros, pieces[2]),
                    (zeros, pieces[3]),
                )
                weights = jnp.concatenate([jnp.concatenate(row, axis=1) for row in rows], axis=0)
            else:
                weights = jnp.concatenate(pieces, axis=0)
            source = jnp.concatenate([x_ref[nbr[j, e]] for j in members], axis=1)
            product = jnp.dot(source, weights, preferred_element_type=jnp.float32)
            for s, j in enumerate(members):
                for k in range(PN):
                    acc[k % 2][ap[j, k, e]] += product[
                        k * half : (k + 1) * half, s * 2 * KB : (s + 1) * 2 * KB
                    ]
        total = acc[0][...] + acc[1][...]
        for one in acc:
            one[...] = jnp.zeros_like(one)
        return total.reshape(QN * half, 2 * KB)

    def project(e, applied):
        xx0, x10, y00, yy0 = doubled(p_ref[e, :, : 2 * KC], low)
        xx1, x11, y01, yy1 = doubled(p_ref[e, :, 2 * KC :], low)
        weights = jnp.concatenate(
            [
                jnp.concatenate([xx0, y00, xx1, y01], axis=1),
                jnp.concatenate([x10, yy0, x11, yy1], axis=1),
            ],
            axis=0,
        )
        contrib = jnp.dot(applied, weights, preferred_element_type=jnp.float32)
        for q in range(QN):
            for k in range(PN):
                parts[k % 2][q % 2][ts[k, q, e]] += contrib[
                    q * half : (q + 1) * half, k * 2 * KC : (k + 1) * 2 * KC
                ]

    def group(i, carry):
        applied = []
        for u in range(GROUP):
            applied.append(apply(i * GROUP + u, accs[u]))
            if carry is None:
                nothing = applied[u][:half] * 0.0
                for part in scratch[2 * GROUP :]:
                    for t in range(u, part.shape[0], GROUP):
                        part[t] = nothing
        for u in range(GROUP):
            project(i * GROUP + u, applied[u].astype(jnp.bfloat16))
        return carry

    for one in scratch[: 2 * GROUP]:
        one[...] = jnp.zeros_like(one)
    group(0, None)
    lax.fori_loop(1, n // GROUP, group, 0)

    def pack(t, carry):
        out_ref[t] = (part_a[t] + part_b[t] + part_c[t] + part_d[t]).astype(jnp.bfloat16)
        return carry

    lax.fori_loop(0, out_ref.shape[0], pack, 0, unroll=8)


def unfolded(first, second):
    rows = [t[:, h * KC : (h + 1) * KC] for t in (first, second) for h in range(2)]
    return jnp.concatenate(rows, axis=0).T


def parcel_kernel(tiles_ref, returned_ref, inbox, send_sem, recv_sem):
    slots = tiles_ref.shape[0] // 9
    barrier = greet()
    pl.semaphore_wait(barrier, 8)
    copies = {}
    for p in ORDER:
        cell = CELLS.index(AROUND[p])
        copies[p] = pltpu.make_async_remote_copy(
            src_ref=tiles_ref.at[pl.ds(cell * slots, slots)],
            dst_ref=inbox.at[pl.ds((8 - cell) * slots, slots)],
            send_sem=send_sem.at[p],
            recv_sem=recv_sem.at[7 - p],
            device_id=device_at(AROUND[p]),
            device_id_type=MESH,
        )
        copies[p].start()

    def settle(source, cell):
        for t in range(cell * slots, (cell + 1) * slots, 2):
            returned_ref[t // 2] = unfolded(source[t], source[t + 1])

    settle(tiles_ref, 4)
    for p in reversed(ORDER):
        copies[p].wait_recv()
        settle(inbox, 8 - CELLS.index(AROUND[p]))
    for p in ORDER:
        copies[p].wait_send()


def owner_kernel(owner_map, returned_ref, out_ref):
    out_ref[...] = jnp.zeros_like(out_ref)
    low = lax.broadcasted_iota(jnp.int32, (KC, 2 * KC), 1) < KC
    right = 1 - low.astype(jnp.int32)
    for t in range(returned_ref.shape[0]):
        pair = returned_ref[t].astype(jnp.float32)
        turned = pltpu.roll(pair, KC, 1)
        both = (jnp.where(low, pair, turned), jnp.where(low, turned, pair))
        for side, tile in enumerate(both):
            m = owner_map[0, 2 * t + side]
            at = pl.ds(pl.multiple_of(lax.shift_right_logical(m, 1) * 2 * KC, 2 * KC), 2 * KC)
            out_ref[:, at] += jnp.where(right == jnp.bitwise_and(m, 1), tile, 0.0)


def body(a_strips, p_strips, nbr_local, ap_slot, tile_slot, send_rows, owner_map):
    width = p_strips.shape[2]
    slots = send_rows.shape[2]
    smem = pl.BlockSpec(memory_space=pltpu.SMEM)
    vmem = pl.BlockSpec(memory_space=pltpu.VMEM)
    tiles_total = owner_map.shape[1]
    n = a_strips.shape[0]
    extended, weights, own_rows = pl.pallas_call(
        ghost_kernel,
        out_shape=(
            jax.ShapeDtypeStruct((n + 8 * slots, 2 * KC, 2 * KB), jnp.bfloat16),
            jax.ShapeDtypeStruct((n, (NB + 1) // 2, 4, KB, 2 * KB), jnp.bfloat16),
            jax.ShapeDtypeStruct(p_strips.shape, p_strips.dtype),
        ),
        in_specs=[pl.BlockSpec(memory_space=pltpu.HBM)] * 3,
        out_specs=(vmem, vmem, vmem),
        scratch_shapes=[
            pltpu.SMEM((slots, 1, 8), jnp.int32),
            pltpu.VMEM(a_strips.shape, a_strips.dtype),
            pltpu.VMEM((8 * slots, KB, width), jnp.bfloat16),
            pltpu.VMEM((8 * slots, KB, width), jnp.bfloat16),
            pltpu.SemaphoreType.DMA((8,)),
            pltpu.SemaphoreType.DMA((8,)),
            pltpu.SemaphoreType.DMA((3,)),
        ],
        compiler_params=pltpu.CompilerParams(collective_id=0, has_side_effects=True, vmem_limit_bytes=24 << 20),
    )(
        pltpu.with_memory_space_constraint(send_rows.transpose(2, 0, 1), pltpu.HBM),
        pltpu.with_memory_space_constraint(p_strips, pltpu.HBM),
        pltpu.with_memory_space_constraint(a_strips, pltpu.HBM),
    )
    tiles = pl.pallas_call(
        local_kernel,
        out_shape=jax.ShapeDtypeStruct((tiles_total, KC // 2, 2 * KC), jnp.bfloat16),
        in_specs=[smem, smem, smem, vmem, vmem, vmem],
        out_specs=vmem,
        scratch_shapes=[pltpu.VMEM((QN, KC // 2, 2 * KB), jnp.float32)] * (2 * GROUP)
        + [pltpu.VMEM((tiles_total, KC // 2, 2 * KC), jnp.float32)] * 4,
        compiler_params=pltpu.CompilerParams(
            vmem_limit_bytes=20 << 20
        ),
    )(
        nbr_local.transpose(1, 0),
        ap_slot.transpose(1, 2, 0),
        tile_slot.transpose(1, 2, 0),
        weights,
        own_rows,
        extended,
    )
    returned = pl.pallas_call(
        parcel_kernel,
        out_shape=jax.ShapeDtypeStruct((tiles_total // 2, KC, 2 * KC), jnp.bfloat16),
        in_specs=[vmem],
        out_specs=vmem,
        scratch_shapes=[
            pltpu.VMEM(tiles.shape, tiles.dtype),
            pltpu.SemaphoreType.DMA((8,)),
            pltpu.SemaphoreType.DMA((8,)),
        ],
        compiler_params=pltpu.CompilerParams(collective_id=1, has_side_effects=True, vmem_limit_bytes=8 << 20),
    )(tiles)
    return pl.pallas_call(
        owner_kernel,
        out_shape=jax.ShapeDtypeStruct((KC, OWN * KC), jnp.float32),
        in_specs=[smem, vmem],
        out_specs=vmem,
        compiler_params=pltpu.CompilerParams(vmem_limit_bytes=8 << 20),
    )(owner_map, returned)


def solution(mesh):
    placed = (
        P(("dom", "grp"), None, None),
        P(("dom", "grp"), None, None),
        P(("dom", "grp"), None),
        P(("dom", "grp"), None, None),
        P(("dom", "grp"), None, None),
        P(("dom", "grp"), None, None),
        P(("dom", "grp"), None),
    )
    return jax.shard_map(
        body, mesh=mesh, in_specs=placed, out_specs=P(None, ("dom", "grp")), check_vma=False
    )
```

```python
import jax
import jax.numpy as jnp
from jax import lax
from jax.experimental import pallas as pl
from jax.experimental.pallas import tpu as pltpu
from jax.sharding import PartitionSpec as P

KB = 64
KC = 64
NB = 7
PN = 4
QN = 8
OWN = 128
GROUP = 8
MESH = pl.DeviceIdType.MESH
CELLS = [(a, b) for a in (-1, 0, 1) for b in (-1, 0, 1)]
AROUND = [cell for cell in CELLS if cell != (0, 0)]
ORDER = sorted(range(8), key=lambda p: -(abs(AROUND[p][0]) * 2 + abs(AROUND[p][1])))
ARRIVALS = ORDER[6:] + ORDER[:6]


def device_at(offset):
    rows, cols = lax.axis_size("dom"), lax.axis_size("grp")
    i = lax.rem(lax.axis_index("dom") + offset[0] + rows, rows)
    j = lax.rem(lax.axis_index("grp") + offset[1] + cols, cols)
    return (i, j)


def greet():
    barrier = pltpu.get_barrier_semaphore()
    for offset in AROUND:
        pl.semaphore_signal(barrier, inc=1, device_id=device_at(offset), device_id_type=MESH)
    return barrier


def folded(x):
    turned = x.T
    half = KC // 2
    blocks = [
        jnp.concatenate(
            [turned[k * KC : k * KC + half], turned[k * KC + half : (k + 1) * KC]], axis=1
        )
        for k in range(PN)
    ]
    return jnp.concatenate(blocks, axis=0)


def doubled(chunk, low):
    zero = jnp.zeros_like(chunk)
    left = jnp.where(low, chunk, zero)
    right = jnp.where(low, zero, chunk)
    return left, pltpu.roll(left, KB, 1), pltpu.roll(right, KB, 1), right


def ghost_kernel(
    rows_hbm,
    p_hbm,
    a_hbm,
    ext_ref,
    weights_ref,
    own_rows,
    send_rows,
    operator,
    own_folded,
    outbox,
    folded_outbox,
    inbox,
    send_sem,
    recv_sem,
    load_sem,
):
    slots = rows_hbm.shape[0]
    n = p_hbm.shape[0]
    loads = (
        pltpu.make_async_copy(rows_hbm, send_rows, load_sem.at[0]),
        pltpu.make_async_copy(p_hbm, own_rows, load_sem.at[1]),
        pltpu.make_async_copy(a_hbm, operator, load_sem.at[2]),
    )
    for load in loads[:2]:
        load.start()
    barrier = greet()
    for load in loads[:2]:
        load.wait()

    def message(p, source, target):
        return pltpu.make_async_remote_copy(
            src_ref=source,
            dst_ref=target,
            send_sem=send_sem.at[p],
            recv_sem=recv_sem.at[7 - p],
            device_id=device_at(AROUND[p]),
            device_id_type=MESH,
        )

    def fill(at, box, rows):
        first = (at % 4) * slots
        for g in range(slots):
            box[first + g] = rows[send_rows[g, 0, ORDER[at]]]

    copies = {}
    for at, p in enumerate(ORDER):
        mine = pl.ds((at % 4) * slots, slots)
        if at < 4:
            place = pl.ds(ORDER.index(7 - p) * slots, slots)
            copies[p] = message(p, outbox.at[mine], inbox.at[place])
        else:
            place = pl.ds(n + (7 - p) * slots, slots)
            copies[p] = message(p, folded_outbox.at[mine], ext_ref.at[place])
    fill(0, outbox, own_rows)
    fill(1, outbox, own_rows)
    pl.semaphore_wait(barrier, 8)
    for at in range(4):
        copies[ORDER[at]].start()
        if at < 2:
            fill(at + 2, outbox, own_rows)
    loads[2].start()

    def fold_own(r, carry):
        row = folded(own_rows[r])
        ext_ref[r] = row
        own_folded[r] = row
        return carry

    lax.fori_loop(0, n, fold_own, 0, unroll=4)
    fill(4, folded_outbox, own_folded)
    fill(5, folded_outbox, own_folded)
    for at in range(4, 8):
        copies[ORDER[at]].start()
        if at < 6:
            fill(at + 2, folded_outbox, own_folded)
    loads[2].wait()
    low = lax.broadcasted_iota(jnp.int32, (KB, 2 * KB), 1) < KB

    def spread(e, carry):
        turned = operator[e].T
        for pair in range((NB + 1) // 2):
            left = turned[2 * pair * KB : (2 * pair + 1) * KB]
            if 2 * pair + 1 < NB:
                right = turned[(2 * pair + 1) * KB : (2 * pair + 2) * KB]
            else:
                right = jnp.zeros_like(left)
            for v, piece in enumerate(doubled(jnp.concatenate([left, right], axis=1), low)):
                weights_ref[e, pair, v] = piece
        return carry

    lax.fori_loop(0, n, spread, 0)
    for p in ARRIVALS:
        copies[p].wait_recv()
        if p in ORDER[:4]:
            for g in range(slots):
                ext_ref[n + (7 - p) * slots + g] = folded(inbox[ORDER.index(7 - p) * slots + g])
    for p in ORDER:
        copies[p].wait_send()


def local_kernel(nbr, ap, ts, a_ref, p_ref, x_ref, out_ref, *scratch):
    n = a_ref.shape[0]
    half = KC // 2
    accs = [scratch[2 * u : 2 * u + 2] for u in range(GROUP)]
    part_a, part_b, part_c, part_d = scratch[2 * GROUP :]
    parts = ((part_a, part_b), (part_c, part_d))
    low = lax.broadcasted_iota(jnp.int32, (KB, 2 * KB), 1) < KB
    zeros = jnp.zeros((KB, 2 * KB), jnp.bfloat16)

    def apply(e, acc):
        for first in range(0, NB, 2):
            members = [j for j in (first, first + 1) if j < NB]
            pieces = [a_ref[e, first // 2, v] for v in range(2 * len(members))]
            if len(members) == 2:
                rows = (
                    (pieces[0], zeros),
                    (pieces[1], zeros),
                    (zeros, pieces[2]),
                    (zeros, pieces[3]),
                )
                weights = jnp.concatenate([jnp.concatenate(row, axis=1) for row in rows], axis=0)
            else:
                weights = jnp.concatenate(pieces, axis=0)
            source = jnp.concatenate([x_ref[nbr[j, e]] for j in members], axis=1)
            product = jnp.dot(source, weights, preferred_element_type=jnp.float32)
            for s, j in enumerate(members):
                for k in range(PN):
                    acc[k % 2][ap[j, k, e]] += product[
                        k * half : (k + 1) * half, s * 2 * KB : (s + 1) * 2 * KB
                    ]
        total = acc[0][...] + acc[1][...]
        for one in acc:
            one[...] = jnp.zeros_like(one)
        return total.reshape(QN * half, 2 * KB)

    def project(e, applied):
        xx0, x10, y00, yy0 = doubled(p_ref[e, :, : 2 * KC], low)
        xx1, x11, y01, yy1 = doubled(p_ref[e, :, 2 * KC :], low)
        weights = jnp.concatenate(
            [
                jnp.concatenate([xx0, y00, xx1, y01], axis=1),
                jnp.concatenate([x10, yy0, x11, yy1], axis=1),
            ],
            axis=0,
        )
        contrib = jnp.dot(applied, weights, preferred_element_type=jnp.float32)
        for q in range(QN):
            for k in range(PN):
                parts[k % 2][q % 2][ts[k, q, e]] += contrib[
                    q * half : (q + 1) * half, k * 2 * KC : (k + 1) * 2 * KC
                ]

    def group(i, carry):
        applied = []
        for u in range(GROUP):
            applied.append(apply(i * GROUP + u, accs[u]))
            if carry is None:
                nothing = applied[u][:half] * 0.0
                for part in scratch[2 * GROUP :]:
                    for t in range(u, part.shape[0], GROUP):
                        part[t] = nothing
        for u in range(GROUP):
            project(i * GROUP + u, applied[u].astype(jnp.bfloat16))
        return carry

    for one in scratch[: 2 * GROUP]:
        one[...] = jnp.zeros_like(one)
    group(0, None)
    lax.fori_loop(1, n // GROUP, group, 0)

    def pack(t, carry):
        out_ref[t] = (part_a[t] + part_b[t] + part_c[t] + part_d[t]).astype(jnp.bfloat16)
        return carry

    lax.fori_loop(0, out_ref.shape[0], pack, 0, unroll=8)


def unfolded(first, second):
    rows = [t[:, h * KC : (h + 1) * KC] for t in (first, second) for h in range(2)]
    return jnp.concatenate(rows, axis=0).T


def parcel_kernel(tiles_ref, returned_ref, inbox, send_sem, recv_sem):
    slots = tiles_ref.shape[0] // 9
    barrier = greet()
    pl.semaphore_wait(barrier, 8)
    copies = {}
    for p in ORDER:
        cell = CELLS.index(AROUND[p])
        copies[p] = pltpu.make_async_remote_copy(
            src_ref=tiles_ref.at[pl.ds(cell * slots, slots)],
            dst_ref=inbox.at[pl.ds((8 - cell) * slots, slots)],
            send_sem=send_sem.at[p],
            recv_sem=recv_sem.at[7 - p],
            device_id=device_at(AROUND[p]),
            device_id_type=MESH,
        )
        copies[p].start()

    def settle(source, cell):
        for t in range(cell * slots, (cell + 1) * slots, 2):
            returned_ref[t // 2] = unfolded(source[t], source[t + 1])

    settle(tiles_ref, 4)
    for p in ARRIVALS:
        copies[p].wait_recv()
        settle(inbox, 8 - CELLS.index(AROUND[p]))
    for p in ORDER:
        copies[p].wait_send()


def owner_kernel(owner_map, returned_ref, out_ref):
    out_ref[...] = jnp.zeros_like(out_ref)
    low = lax.broadcasted_iota(jnp.int32, (KC, 2 * KC), 1) < KC
    right = 1 - low.astype(jnp.int32)
    for t in range(returned_ref.shape[0]):
        pair = returned_ref[t].astype(jnp.float32)
        turned = pltpu.roll(pair, KC, 1)
        both = (jnp.where(low, pair, turned), jnp.where(low, turned, pair))
        for side, tile in enumerate(both):
            m = owner_map[0, 2 * t + side]
            at = pl.ds(pl.multiple_of(lax.shift_right_logical(m, 1) * 2 * KC, 2 * KC), 2 * KC)
            out_ref[:, at] += jnp.where(right == jnp.bitwise_and(m, 1), tile, 0.0)


def body(a_strips, p_strips, nbr_local, ap_slot, tile_slot, send_rows, owner_map):
    width = p_strips.shape[2]
    slots = send_rows.shape[2]
    smem = pl.BlockSpec(memory_space=pltpu.SMEM)
    vmem = pl.BlockSpec(memory_space=pltpu.VMEM)
    tiles_total = owner_map.shape[1]
    n = a_strips.shape[0]
    extended, weights, own_rows = pl.pallas_call(
        ghost_kernel,
        out_shape=(
            jax.ShapeDtypeStruct((n + 8 * slots, 2 * KC, 2 * KB), jnp.bfloat16),
            jax.ShapeDtypeStruct((n, (NB + 1) // 2, 4, KB, 2 * KB), jnp.bfloat16),
            jax.ShapeDtypeStruct(p_strips.shape, p_strips.dtype),
        ),
        in_specs=[pl.BlockSpec(memory_space=pltpu.HBM)] * 3,
        out_specs=(vmem, vmem, vmem),
        scratch_shapes=[
            pltpu.SMEM((slots, 1, 8), jnp.int32),
            pltpu.VMEM(a_strips.shape, a_strips.dtype),
            pltpu.VMEM((n, 2 * KC, 2 * KB), jnp.bfloat16),
            pltpu.VMEM((4 * slots, KB, width), jnp.bfloat16),
            pltpu.VMEM((4 * slots, 2 * KC, 2 * KB), jnp.bfloat16),
            pltpu.VMEM((4 * slots, KB, width), jnp.bfloat16),
            pltpu.SemaphoreType.DMA((8,)),
            pltpu.SemaphoreType.DMA((8,)),
            pltpu.SemaphoreType.DMA((3,)),
        ],
        compiler_params=pltpu.CompilerParams(collective_id=0, has_side_effects=True, vmem_limit_bytes=24 << 20),
    )(
        pltpu.with_memory_space_constraint(send_rows.transpose(2, 0, 1), pltpu.HBM),
        pltpu.with_memory_space_constraint(p_strips, pltpu.HBM),
        pltpu.with_memory_space_constraint(a_strips, pltpu.HBM),
    )
    tiles = pl.pallas_call(
        local_kernel,
        out_shape=jax.ShapeDtypeStruct((tiles_total, KC // 2, 2 * KC), jnp.bfloat16),
        in_specs=[smem, smem, smem, vmem, vmem, vmem],
        out_specs=vmem,
        scratch_shapes=[pltpu.VMEM((QN, KC // 2, 2 * KB), jnp.float32)] * (2 * GROUP)
        + [pltpu.VMEM((tiles_total, KC // 2, 2 * KC), jnp.float32)] * 4,
        compiler_params=pltpu.CompilerParams(
            vmem_limit_bytes=20 << 20
        ),
    )(
        nbr_local.transpose(1, 0),
        ap_slot.transpose(1, 2, 0),
        tile_slot.transpose(1, 2, 0),
        weights,
        own_rows,
        extended,
    )
    returned = pl.pallas_call(
        parcel_kernel,
        out_shape=jax.ShapeDtypeStruct((tiles_total // 2, KC, 2 * KC), jnp.bfloat16),
        in_specs=[vmem],
        out_specs=vmem,
        scratch_shapes=[
            pltpu.VMEM(tiles.shape, tiles.dtype),
            pltpu.SemaphoreType.DMA((8,)),
            pltpu.SemaphoreType.DMA((8,)),
        ],
        compiler_params=pltpu.CompilerParams(collective_id=1, has_side_effects=True, vmem_limit_bytes=8 << 20),
    )(tiles)
    return pl.pallas_call(
        owner_kernel,
        out_shape=jax.ShapeDtypeStruct((KC, OWN * KC), jnp.float32),
        in_specs=[smem, vmem],
        out_specs=vmem,
        compiler_params=pltpu.CompilerParams(vmem_limit_bytes=8 << 20),
    )(owner_map, returned)


def solution(mesh):
    placed = (
        P(("dom", "grp"), None, None),
        P(("dom", "grp"), None, None),
        P(("dom", "grp"), None),
        P(("dom", "grp"), None, None),
        P(("dom", "grp"), None, None),
        P(("dom", "grp"), None, None),
        P(("dom", "grp"), None),
    )
    return jax.shard_map(
        body, mesh=mesh, in_specs=placed, out_specs=P(None, ("dom", "grp")), check_vma=False
    )
```

```python
import jax
import jax.numpy as jnp
from jax import lax
from jax.experimental import pallas as pl
from jax.experimental.pallas import tpu as pltpu
from jax.sharding import PartitionSpec as P

KB = 64
KC = 64
NB = 7
PN = 4
QN = 8
OWN = 128
GROUP = 8
MESH = pl.DeviceIdType.MESH
CELLS = [(a, b) for a in (-1, 0, 1) for b in (-1, 0, 1)]
AROUND = [cell for cell in CELLS if cell != (0, 0)]
ORDER = sorted(range(8), key=lambda p: -(abs(AROUND[p][0]) * 2 + abs(AROUND[p][1])))
ARRIVALS = ORDER[6:] + ORDER[:6]


def device_at(offset):
    rows, cols = lax.axis_size("dom"), lax.axis_size("grp")
    i = lax.rem(lax.axis_index("dom") + offset[0] + rows, rows)
    j = lax.rem(lax.axis_index("grp") + offset[1] + cols, cols)
    return (i, j)


def greet():
    barrier = pltpu.get_barrier_semaphore()
    for offset in AROUND:
        pl.semaphore_signal(barrier, inc=1, device_id=device_at(offset), device_id_type=MESH)
    return barrier


def folded(x):
    turned = x.T
    half = KC // 2
    blocks = [
        jnp.concatenate(
            [turned[k * KC : k * KC + half], turned[k * KC + half : (k + 1) * KC]], axis=1
        )
        for k in range(PN)
    ]
    return jnp.concatenate(blocks, axis=0)


def doubled(chunk, low):
    zero = jnp.zeros_like(chunk)
    left = jnp.where(low, chunk, zero)
    right = jnp.where(low, zero, chunk)
    return left, pltpu.roll(left, KB, 1), pltpu.roll(right, KB, 1), right


def ghost_kernel(
    rows_hbm,
    p_hbm,
    a_hbm,
    ext_ref,
    weights_ref,
    own_rows,
    self_ref,
    send_rows,
    operator,
    own_folded,
    outbox,
    folded_outbox,
    inbox,
    send_sem,
    recv_sem,
    load_sem,
):
    slots = rows_hbm.shape[0]
    n = p_hbm.shape[0]
    loads = (
        pltpu.make_async_copy(rows_hbm, send_rows, load_sem.at[0]),
        pltpu.make_async_copy(p_hbm, own_rows, load_sem.at[1]),
        pltpu.make_async_copy(a_hbm, operator, load_sem.at[2]),
    )
    for load in loads[:2]:
        load.start()
    barrier = greet()
    for load in loads[:2]:
        load.wait()

    def message(p, source, target):
        return pltpu.make_async_remote_copy(
            src_ref=source,
            dst_ref=target,
            send_sem=send_sem.at[p],
            recv_sem=recv_sem.at[7 - p],
            device_id=device_at(AROUND[p]),
            device_id_type=MESH,
        )

    def fill(at, box, rows):
        first = (at % 4) * slots
        for g in range(slots):
            box[first + g] = rows[send_rows[g, 0, ORDER[at]]]

    copies = {}
    for at, p in enumerate(ORDER):
        mine = pl.ds((at % 4) * slots, slots)
        if at < 4:
            place = pl.ds(ORDER.index(7 - p) * slots, slots)
            copies[p] = message(p, outbox.at[mine], inbox.at[place])
        else:
            place = pl.ds(n + (7 - p) * slots, slots)
            copies[p] = message(p, folded_outbox.at[mine], ext_ref.at[place])
    fill(0, outbox, own_rows)
    fill(1, outbox, own_rows)
    pl.semaphore_wait(barrier, 8)
    for at in range(4):
        copies[ORDER[at]].start()
        if at < 2:
            fill(at + 2, outbox, own_rows)
    loads[2].start()

    def fold_own(r, carry):
        row = folded(own_rows[r])
        ext_ref[r] = row
        own_folded[r] = row
        return carry

    lax.fori_loop(0, n, fold_own, 0, unroll=4)
    fill(4, folded_outbox, own_folded)
    fill(5, folded_outbox, own_folded)
    for at in range(4, 8):
        copies[ORDER[at]].start()
        if at < 6:
            fill(at + 2, folded_outbox, own_folded)
    loads[2].wait()
    low = lax.broadcasted_iota(jnp.int32, (KB, 2 * KB), 1) < KB

    def spread(e, carry):
        turned = operator[e].T
        blocks = [turned[j * KB : (j + 1) * KB] for j in range(NB)]
        for pair in range(NB // 2):
            both = jnp.concatenate(blocks[2 * pair + 1 : 2 * pair + 3], axis=1)
            for v, piece in enumerate(doubled(both, low)):
                weights_ref[e, pair, v] = piece
        none = jnp.zeros_like(blocks[0])
        left, shifted = doubled(jnp.concatenate([blocks[0], none], axis=1), low)[:2]
        self_ref[e] = jnp.dot(
            own_folded[e],
            jnp.concatenate([left, shifted], axis=0),
            preferred_element_type=jnp.float32,
        )
        return carry

    lax.fori_loop(0, n, spread, 0)
    for p in ARRIVALS:
        copies[p].wait_recv()
        if p in ORDER[:4]:
            for g in range(slots):
                ext_ref[n + (7 - p) * slots + g] = folded(inbox[ORDER.index(7 - p) * slots + g])
    for p in ORDER:
        copies[p].wait_send()


def local_kernel(nbr, ap, ts, self_ref, a_ref, p_ref, x_ref, out_ref, *scratch):
    n = a_ref.shape[0]
    half = KC // 2
    accs = [scratch[2 * u : 2 * u + 2] for u in range(GROUP)]
    part_a, part_b, part_c, part_d = scratch[2 * GROUP :]
    parts = ((part_a, part_b), (part_c, part_d))
    low = lax.broadcasted_iota(jnp.int32, (KB, 2 * KB), 1) < KB
    zeros = jnp.zeros((KB, 2 * KB), jnp.bfloat16)

    def add(e, acc, j, product):
        for k in range(PN):
            acc[k % 2][ap[j, k, e]] += product[k * half : (k + 1) * half]

    def apply(e, acc):
        for first in range(1, NB, 2):
            pieces = [a_ref[e, first // 2, v] for v in range(4)]
            rows = (
                (pieces[0], zeros),
                (pieces[1], zeros),
                (zeros, pieces[2]),
                (zeros, pieces[3]),
            )
            weights = jnp.concatenate([jnp.concatenate(row, axis=1) for row in rows], axis=0)
            source = jnp.concatenate([x_ref[nbr[j, e]] for j in (first, first + 1)], axis=1)
            product = jnp.dot(source, weights, preferred_element_type=jnp.float32)
            for j in (first, first + 1):
                add(e, acc, j, product[:, (j - first) * 2 * KB : (j - first + 1) * 2 * KB])
        add(e, acc, 0, self_ref[e])
        total = acc[0][...] + acc[1][...]
        for one in acc:
            one[...] = jnp.zeros_like(one)
        return total.reshape(QN * half, 2 * KB)

    def project(e, applied):
        xx0, x10, y00, yy0 = doubled(p_ref[e, :, : 2 * KC], low)
        xx1, x11, y01, yy1 = doubled(p_ref[e, :, 2 * KC :], low)
        weights = jnp.concatenate(
            [
                jnp.concatenate([xx0, y00, xx1, y01], axis=1),
                jnp.concatenate([x10, yy0, x11, yy1], axis=1),
            ],
            axis=0,
        )
        contrib = jnp.dot(applied, weights, preferred_element_type=jnp.float32)
        for q in range(QN):
            for k in range(PN):
                parts[k % 2][q % 2][ts[k, q, e]] += contrib[
                    q * half : (q + 1) * half, k * 2 * KC : (k + 1) * 2 * KC
                ]

    def group(i, carry):
        applied = []
        for u in range(GROUP):
            applied.append(apply(i * GROUP + u, accs[u]))
            if carry is None:
                nothing = applied[u][:half] * 0.0
                for part in scratch[2 * GROUP :]:
                    for t in range(u, part.shape[0], GROUP):
                        part[t] = nothing
        for u in range(GROUP):
            project(i * GROUP + u, applied[u].astype(jnp.bfloat16))
        return carry

    for one in scratch[: 2 * GROUP]:
        one[...] = jnp.zeros_like(one)
    group(0, None)
    lax.fori_loop(1, n // GROUP, group, 0)

    def pack(t, carry):
        out_ref[t] = (part_a[t] + part_b[t] + part_c[t] + part_d[t]).astype(jnp.bfloat16)
        return carry

    lax.fori_loop(0, out_ref.shape[0], pack, 0, unroll=8)


def unfolded(first, second):
    rows = [t[:, h * KC : (h + 1) * KC] for t in (first, second) for h in range(2)]
    return jnp.concatenate(rows, axis=0).T


def parcel_kernel(tiles_ref, returned_ref, inbox, send_sem, recv_sem):
    slots = tiles_ref.shape[0] // 9
    barrier = greet()
    pl.semaphore_wait(barrier, 8)
    copies = {}
    for p in ORDER:
        cell = CELLS.index(AROUND[p])
        copies[p] = pltpu.make_async_remote_copy(
            src_ref=tiles_ref.at[pl.ds(cell * slots, slots)],
            dst_ref=inbox.at[pl.ds((8 - cell) * slots, slots)],
            send_sem=send_sem.at[p],
            recv_sem=recv_sem.at[7 - p],
            device_id=device_at(AROUND[p]),
            device_id_type=MESH,
        )
        copies[p].start()

    def settle(source, cell):
        for t in range(cell * slots, (cell + 1) * slots, 2):
            returned_ref[t // 2] = unfolded(source[t], source[t + 1])

    settle(tiles_ref, 4)
    for p in ARRIVALS:
        copies[p].wait_recv()
        settle(inbox, 8 - CELLS.index(AROUND[p]))
    for p in ORDER:
        copies[p].wait_send()


def owner_kernel(owner_map, returned_ref, out_ref):
    out_ref[...] = jnp.zeros_like(out_ref)
    low = lax.broadcasted_iota(jnp.int32, (KC, 2 * KC), 1) < KC
    right = 1 - low.astype(jnp.int32)
    for t in range(returned_ref.shape[0]):
        pair = returned_ref[t].astype(jnp.float32)
        turned = pltpu.roll(pair, KC, 1)
        both = (jnp.where(low, pair, turned), jnp.where(low, turned, pair))
        for side, tile in enumerate(both):
            m = owner_map[0, 2 * t + side]
            at = pl.ds(pl.multiple_of(lax.shift_right_logical(m, 1) * 2 * KC, 2 * KC), 2 * KC)
            out_ref[:, at] += jnp.where(right == jnp.bitwise_and(m, 1), tile, 0.0)


def body(a_strips, p_strips, nbr_local, ap_slot, tile_slot, send_rows, owner_map):
    width = p_strips.shape[2]
    slots = send_rows.shape[2]
    smem = pl.BlockSpec(memory_space=pltpu.SMEM)
    vmem = pl.BlockSpec(memory_space=pltpu.VMEM)
    tiles_total = owner_map.shape[1]
    n = a_strips.shape[0]
    extended, weights, own_rows, own_products = pl.pallas_call(
        ghost_kernel,
        out_shape=(
            jax.ShapeDtypeStruct((n + 8 * slots, 2 * KC, 2 * KB), jnp.bfloat16),
            jax.ShapeDtypeStruct((n, NB // 2, 4, KB, 2 * KB), jnp.bfloat16),
            jax.ShapeDtypeStruct(p_strips.shape, p_strips.dtype),
            jax.ShapeDtypeStruct((n, 2 * KC, 2 * KB), jnp.float32),
        ),
        in_specs=[pl.BlockSpec(memory_space=pltpu.HBM)] * 3,
        out_specs=(vmem, vmem, vmem, vmem),
        scratch_shapes=[
            pltpu.SMEM((slots, 1, 8), jnp.int32),
            pltpu.VMEM(a_strips.shape, a_strips.dtype),
            pltpu.VMEM((n, 2 * KC, 2 * KB), jnp.bfloat16),
            pltpu.VMEM((4 * slots, KB, width), jnp.bfloat16),
            pltpu.VMEM((4 * slots, 2 * KC, 2 * KB), jnp.bfloat16),
            pltpu.VMEM((4 * slots, KB, width), jnp.bfloat16),
            pltpu.SemaphoreType.DMA((8,)),
            pltpu.SemaphoreType.DMA((8,)),
            pltpu.SemaphoreType.DMA((3,)),
        ],
        compiler_params=pltpu.CompilerParams(collective_id=0, has_side_effects=True, vmem_limit_bytes=24 << 20),
    )(
        pltpu.with_memory_space_constraint(send_rows.transpose(2, 0, 1), pltpu.HBM),
        pltpu.with_memory_space_constraint(p_strips, pltpu.HBM),
        pltpu.with_memory_space_constraint(a_strips, pltpu.HBM),
    )
    tiles = pl.pallas_call(
        local_kernel,
        out_shape=jax.ShapeDtypeStruct((tiles_total, KC // 2, 2 * KC), jnp.bfloat16),
        in_specs=[smem, smem, smem, vmem, vmem, vmem, vmem],
        out_specs=vmem,
        scratch_shapes=[pltpu.VMEM((QN, KC // 2, 2 * KB), jnp.float32)] * (2 * GROUP)
        + [pltpu.VMEM((tiles_total, KC // 2, 2 * KC), jnp.float32)] * 4,
        compiler_params=pltpu.CompilerParams(
            vmem_limit_bytes=26 << 20
        ),
    )(
        nbr_local.transpose(1, 0),
        ap_slot.transpose(1, 2, 0),
        tile_slot.transpose(1, 2, 0),
        own_products,
        weights,
        own_rows,
        extended,
    )
    returned = pl.pallas_call(
        parcel_kernel,
        out_shape=jax.ShapeDtypeStruct((tiles_total // 2, KC, 2 * KC), jnp.bfloat16),
        in_specs=[vmem],
        out_specs=vmem,
        scratch_shapes=[
            pltpu.VMEM(tiles.shape, tiles.dtype),
            pltpu.SemaphoreType.DMA((8,)),
            pltpu.SemaphoreType.DMA((8,)),
        ],
        compiler_params=pltpu.CompilerParams(collective_id=1, has_side_effects=True, vmem_limit_bytes=8 << 20),
    )(tiles)
    return pl.pallas_call(
        owner_kernel,
        out_shape=jax.ShapeDtypeStruct((KC, OWN * KC), jnp.float32),
        in_specs=[smem, vmem],
        out_specs=vmem,
        compiler_params=pltpu.CompilerParams(vmem_limit_bytes=8 << 20),
    )(owner_map, returned)


def solution(mesh):
    placed = (
        P(("dom", "grp"), None, None),
        P(("dom", "grp"), None, None),
        P(("dom", "grp"), None),
        P(("dom", "grp"), None, None),
        P(("dom", "grp"), None, None),
        P(("dom", "grp"), None, None),
        P(("dom", "grp"), None),
    )
    return jax.shard_map(
        body, mesh=mesh, in_specs=placed, out_specs=P(None, ("dom", "grp")), check_vma=False
    )
```
